256 devices in a mesh: cls: 8 (over x, core), dom: 32 (over z, y).
Axes of the slice: x: 4, y: 4, z: 8, core: 2. Of those that a mesh axis runs over, the one named last changes fastest.
Arguments:
- particles: bfloat16 [1024, 36864], P(('cls', 'dom')), may hold values from -6 to 6
- references: bfloat16 [200, 36864], P('cls'), may hold values from -0.03125 to 0.03125
- candidates: int32 [1024, 8], P(('cls', 'dom')), may hold values from 0 to 199, as said below
- offsets: int32 [1024, 2], P(('cls', 'dom')), may hold values from -7 to 7
Outputs:
- class_average: bfloat16 [200, 36864], P('cls')
The draws below stay inside these ranges and needn't reach their ends.
Inputs may be any that keep to these rules, and one draw needn't show every extreme that they name: `candidates`: each particle lists 8 distinct classes, 4 of them with each of two class owners, the owner of class c being c // (200 / number of cls groups). Of the 4 particles of one device at most 2 list classes of one owner, and on every device some owner is listed by exactly 2.
All inputs are finite; a program needn't handle non-finite values.
Results may differ from the reference program's by a relative error of at most 0.0074.
Values may be sent and summed in bfloat16 or wider, within the bound.
A program may use at most 128 MiB of HBM per device.

```python
import math
import jax
import jax.numpy as jnp
from jax import lax

CLASSES = 200
CYCLES = 128
ANGLES = 144
ROT = 36
SHIFTS = 5
CAND = 8
BOX = 256
PART_DEV = 4
CAP = 2
CLS_LOC = 25
PIXV = 36864
PARTICLES = 1024
N_CLS = 8


def route_tables(key):
    block_list = PARTICLES // PART_DEV
    half_count = CAND // 2

    def one_block(block_key):
        subkeys = jax.random.split(block_key, 6)
        owner_list = jax.random.permutation(subkeys[0], N_CLS)
        ordering = jax.random.permutation(subkeys[1], PART_DEV)
        first_owner = owner_list[ordering // CAP]
        second_owner = owner_list[2 + ordering % (N_CLS - 2)]
        pick_first = jax.vmap(lambda sub_key: jax.random.permutation(sub_key, CLS_LOC)[:half_count])(jax.random.split(subkeys[2], PART_DEV))
        pick_second = jax.vmap(lambda sub_key: jax.random.permutation(sub_key, CLS_LOC)[:half_count])(jax.random.split(subkeys[3], PART_DEV))
        listed = jnp.concatenate([first_owner[:, None] * CLS_LOC + pick_first, second_owner[:, None] * CLS_LOC + pick_second], axis=1)
        mixing = jax.vmap(lambda sub_key: jax.random.permutation(sub_key, CAND))(jax.random.split(subkeys[4], PART_DEV))
        shuffled = jnp.take_along_axis(listed, mixing, axis=1)
        prior_shift = jax.random.randint(subkeys[5], (PART_DEV, 2), -7, 8, dtype=jnp.int32)
        return (shuffled, prior_shift, listed[:, 0])
    shuffled, prior_shift, leading = jax.vmap(one_block)(jax.random.split(jax.random.fold_in(key, 11), block_list))
    return (shuffled.reshape(PARTICLES, CAND), prior_shift.reshape(PARTICLES, 2))


def reference_field(key):
    base_key = jax.random.fold_in(key, 29)
    field = jnp.clip(jax.random.normal(base_key, (CLASSES, ANGLES, 2, CYCLES), jnp.float32), -6.0, 6.0) * PIXV ** (-0.5)
    return field


def draw_references(key, part):
    return reference_field(key).reshape(CLASSES, PIXV).astype(jnp.bfloat16)


def draw_candidates(key, part):
    return route_tables(key)[0]


def draw_offsets(key, part):
    return route_tables(key)[1]


def draw_particles(key, part):
    base_key = jax.random.fold_in(key, 37)
    values = jnp.clip(jax.random.normal(base_key, (PARTICLES, ANGLES, 2, CYCLES), jnp.float32), -6.0, 6.0)
    return values.reshape(PARTICLES, PIXV).astype(jnp.bfloat16)


def setup_inputs(seed: int = 0) -> dict:
    arg_keys = jax.random.split(jax.random.key(seed), 5)
    particles = draw_particles(jax.random.fold_in(arg_keys[4], 71), 0)
    references = draw_references(jax.random.fold_in(arg_keys[4], 71), 0)
    candidates = draw_candidates(jax.random.fold_in(arg_keys[4], 71), 0)
    offsets = draw_offsets(jax.random.fold_in(arg_keys[4], 71), 0)
    return {"particles": particles, "references": references, "candidates": candidates, "offsets": offsets}


SOFTMAX_WARMTH = 2.0
PRIOR_MASS = 1.0
SHIFT_X_STEPS = (0, 1, -1, 0, 0)
SHIFT_Y_STEPS = (0, 0, 0, 1, -1)


def phase_angles(move_x, move_y):
    theta = 2.0 * math.pi * jnp.arange(ANGLES, dtype=jnp.float32) / ANGLES
    radius = jnp.arange(1, CYCLES + 1, dtype=jnp.float32)
    along = jnp.cos(theta)[:, None] * move_x.astype(jnp.float32)[..., None, None] + jnp.sin(theta)[:, None] * move_y.astype(jnp.float32)[..., None, None]
    return (2.0 * math.pi / BOX) * along * radius


def shift_images(images, phase):
    real_part = images[..., 0, :].astype(jnp.float32)
    imag_part = images[..., 1, :].astype(jnp.float32)
    cosine = jnp.cos(phase)
    sine = jnp.sin(phase)
    return jnp.stack([real_part * cosine + imag_part * sine, imag_part * cosine - real_part * sine], axis=-2).astype(jnp.bfloat16)


def reference(particles, references, candidates, offsets):
    block_width = PIXV // ROT
    turn_index = jnp.arange(ROT, dtype=jnp.int32)
    source_block = (turn_index[:, None] + turn_index[None, :]) % ROT
    steps_x = jnp.array(SHIFT_X_STEPS, dtype=jnp.int32)
    steps_y = jnp.array(SHIFT_Y_STEPS, dtype=jnp.int32)

    def one_particle(carry, element):
        totals, masses = carry
        particle_image, listed, prior_shift = element
        phase = phase_angles(prior_shift[0] + steps_x, prior_shift[1] + steps_y)
        shifted = shift_images(particle_image.reshape(ANGLES, 2, CYCLES)[None], phase)
        shifted = shifted.reshape(SHIFTS, ROT, block_width)
        rotated_images = shifted[:, source_block, :].reshape(SHIFTS * ROT, PIXV)
        selected_candidates = references[listed]
        score_values = SOFTMAX_WARMTH * jnp.dot(rotated_images, selected_candidates.T, preferred_element_type=jnp.float32)
        best_score = jnp.max(score_values)
        exponent = jnp.exp(score_values - best_score)
        weight = (exponent / jnp.sum(exponent)).astype(jnp.bfloat16)
        contrib = jnp.dot(weight.T, rotated_images, preferred_element_type=jnp.float32)
        totals = totals.at[listed].add(contrib)
        masses = masses.at[listed].add(jnp.sum(weight.astype(jnp.float32), axis=0))
        return (totals, masses), None

    initial = (jnp.zeros((CLASSES, PIXV), jnp.float32), jnp.zeros((CLASSES,), jnp.float32))
    (totals, masses), unused = lax.scan(one_particle, initial, (particles, candidates, offsets))
    return (totals / (masses + PRIOR_MASS)[:, None]).astype(jnp.bfloat16)
```

```python
import math

import jax
import jax.numpy as jnp
from jax import lax
from jax.experimental import pallas as pl
from jax.experimental.pallas import tpu as pltpu
from jax.sharding import PartitionSpec as P

MESH = pl.DeviceIdType.MESH
CYCLES = 128
ANGLES = 144
ROT = 36
SHIFTS = 5
BOX = 256
NCH, RC = 3, 80
LEAD, DROWS = 15, 225
CLS_LOC, ROTS = 25, 36


SOFTMAX_WARMTH = 2.0
PRIOR_MASS = 1.0
NEGATIVE = -1e30
SHIFT_X_STEPS = (0, 1, -1, 0, 0)
SHIFT_Y_STEPS = (0, 0, 0, 1, -1)


def phase_angles(move_x, move_y):
    theta = 2.0 * math.pi * jnp.arange(ANGLES, dtype=jnp.float32) / ANGLES
    radius = jnp.arange(1, CYCLES + 1, dtype=jnp.float32)
    along = (
        jnp.cos(theta)[:, None] * move_x.astype(jnp.float32)[..., None, None]
        + jnp.sin(theta)[:, None] * move_y.astype(jnp.float32)[..., None, None]
    )
    return 2.0 * math.pi / BOX * along * radius


def shift_images(images, phase):
    real_part = images[..., 0, :].astype(jnp.float32)
    imag_part = images[..., 1, :].astype(jnp.float32)
    cosine = jnp.cos(phase)
    sine = jnp.sin(phase)
    return jnp.stack(
        [real_part * cosine + imag_part * sine, imag_part * cosine - real_part * sine], axis=-2
    ).astype(jnp.bfloat16)


def reduce_kernel(p_ref, g_ref, x1, x2, d3, d4, e5, e6, c1, c2, s_buf, z_buf, ysend, yrecv, zsend, zrecv):
    dom = lax.axis_index("dom")
    y = dom % 4
    z = dom // 4
    yp, ym, yo = (y + 1) % 4, (y + 3) % 4, (y + 2) % 4
    up, down = {"dom": z * 4 + yp}, {"dom": z * 4 + ym}
    zdev = [{"dom": ((z + k) % 8) * 4 + y} for k in range(8)]
    barrier = pltpu.get_barrier_semaphore()
    for target in [up, down] + zdev[1:]:
        pl.semaphore_signal(barrier, inc=1, device_id=target, device_id_type=MESH)
    pl.semaphore_wait(barrier, 9)
    A, B = pl.ds(0, 4), pl.ds(4, 4)

    def send(src, dst, ssem, rsem, target):
        copy = pltpu.make_async_remote_copy(src_ref=src, dst_ref=dst, send_sem=ssem, recv_sem=rsem,
                                            device_id=target, device_id_type=MESH)
        copy.start()
        return copy

    pending = []
    m1, m2, m3, m4, m5, m6 = {}, {}, {}, {}, {}, {}
    for ch in range(NCH):
        m1[ch] = send(p_ref.at[ch, yo, A], x1.at[ch], ysend.at[ch, 0], yrecv.at[ch, 0], up)
        m2[ch] = send(p_ref.at[ch, yo, B], x2.at[ch], ysend.at[ch, 1], yrecv.at[ch, 1], down)
        m3[ch] = send(p_ref.at[ch, yp, B], d3.at[ch], ysend.at[ch, 2], yrecv.at[ch, 2], up)
        m4[ch] = send(p_ref.at[ch, ym, A], d4.at[ch], ysend.at[ch, 3], yrecv.at[ch, 3], down)
    for ch in range(NCH):
        m1[ch].wait_recv()
        c1[ch] = (x1[ch].astype(jnp.float32) + p_ref[ch, yp, A].astype(jnp.float32)).astype(jnp.bfloat16)
        m5[ch] = send(c1.at[ch], e5.at[ch], ysend.at[ch, 4], yrecv.at[ch, 4], up)
        m2[ch].wait_recv()
        c2[ch] = (x2[ch].astype(jnp.float32) + p_ref[ch, ym, B].astype(jnp.float32)).astype(jnp.bfloat16)
        m6[ch] = send(c2.at[ch], e6.at[ch], ysend.at[ch, 5], yrecv.at[ch, 5], down)
    zm = {}
    for ch in range(NCH):
        m4[ch].wait_recv()
        m5[ch].wait_recv()
        s_buf[ch, A] = (p_ref[ch, y, A].astype(jnp.float32) + e5[ch].astype(jnp.float32)
                        + d4[ch].astype(jnp.float32)).astype(jnp.bfloat16)
        m3[ch].wait_recv()
        m6[ch].wait_recv()
        s_buf[ch, B] = (p_ref[ch, y, B].astype(jnp.float32) + e6[ch].astype(jnp.float32)
                        + d3[ch].astype(jnp.float32)).astype(jnp.bfloat16)
        for k in range(1, 8):
            zm[ch, k] = send(s_buf.at[ch, (z + k) % 8], z_buf.at[ch, k - 1],
                             zsend.at[ch, k - 1], zrecv.at[ch, k - 1], zdev[k])
    zg = {}
    mass = None
    for ch in range(NCH):
        num = s_buf[ch, z].astype(jnp.float32)
        for k in range(1, 8):
            zm[ch, k].wait_recv()
            num = num + z_buf[ch, k - 1].astype(jnp.float32)
        if ch == 0:
            mass = num[0:1, :] + num[1:2, :] + 1.0
        place = DROWS * y + (ch * RC - LEAD) + lax.broadcasted_iota(jnp.int32, (RC, 128), 0)
        den = jnp.ones((RC, 128), jnp.float32)
        for c in range(CLS_LOC):
            here = (place >= c * ROTS) & (place < (c + 1) * ROTS)
            den = jnp.where(here, jnp.broadcast_to(mass[:, c:c + 1], (RC, 128)), den)
        g_ref[ch, y, z] = (num / den).astype(jnp.bfloat16)
        for k in range(1, 8):
            zg[ch, k] = send(g_ref.at[ch, y, z], g_ref.at[ch, y, z],
                             zsend.at[ch, 6 + k], zrecv.at[ch, 6 + k], zdev[k])
    m7, m8, m9, m10 = {}, {}, {}, {}
    for ch in range(NCH):
        for k in range(1, 8):
            zg[ch, k].wait_recv()
        m7[ch] = send(g_ref.at[ch, y], g_ref.at[ch, y], ysend.at[ch, 6], yrecv.at[ch, 6], up)
        m8[ch] = send(g_ref.at[ch, y], g_ref.at[ch, y], ysend.at[ch, 7], yrecv.at[ch, 7], down)
    for ch in range(NCH):
        m7[ch].wait_recv()
        m9[ch] = send(g_ref.at[ch, ym, A], g_ref.at[ch, ym, A], ysend.at[ch, 8], yrecv.at[ch, 8], up)
        m8[ch].wait_recv()
        m10[ch] = send(g_ref.at[ch, yp, B], g_ref.at[ch, yp, B], ysend.at[ch, 9], yrecv.at[ch, 9], down)
    for ch in range(NCH):
        m9[ch].wait_recv()
        m10[ch].wait_recv()
    for group in (m1, m2, m3, m4, m5, m6, zm, zg, m7, m8, m9, m10):
        for copy in group.values():
            copy.wait_send()


def reduce_average(payload):
    half = pltpu.VMEM((NCH, 4, RC, 128), jnp.bfloat16)
    return pl.pallas_call(
        reduce_kernel,
        out_shape=jax.ShapeDtypeStruct((NCH, 4, 8, RC, 128), jnp.bfloat16),
        in_specs=[pl.BlockSpec(memory_space=pltpu.VMEM)],
        out_specs=pl.BlockSpec(memory_space=pltpu.VMEM),
        scratch_shapes=[half] * 8 + [
            pltpu.VMEM((NCH, 8, RC, 128), jnp.bfloat16),
            pltpu.VMEM((NCH, 7, RC, 128), jnp.bfloat16),
            pltpu.SemaphoreType.DMA((NCH, 10)),
            pltpu.SemaphoreType.DMA((NCH, 10)),
            pltpu.SemaphoreType.DMA((NCH, 14)),
            pltpu.SemaphoreType.DMA((NCH, 14)),
        ],
        compiler_params=pltpu.CompilerParams(collective_id=5, has_side_effects=True, vmem_limit_bytes=40 << 20),
        name="reduce_average",
    )(payload)


def pack_payload(totals, masses):
    rows = totals.reshape(4, DROWS, 8, 128)
    hi = masses.astype(jnp.bfloat16).astype(jnp.float32)
    lead = jnp.pad(jnp.stack([hi, masses - hi]), ((0, LEAD - 2), (0, 128 - CLS_LOC)))
    lead = jnp.broadcast_to(lead[None, :, None, :], (4, LEAD, 8, 128))
    whole = jnp.concatenate([lead, rows], axis=1).astype(jnp.bfloat16)
    return whole.reshape(4, NCH, RC, 8, 128).transpose(1, 0, 3, 2, 4)


def unpack_average(gathered):
    rows = gathered.transpose(1, 0, 3, 2, 4).reshape(4, NCH * RC, 8, 128)[:, LEAD:]
    return rows.reshape(CLS_LOC, 36864)


def shards(particles, references, candidates, offsets):
    groups = lax.axis_size("cls")
    owner = lax.axis_index("cls")
    count = particles.shape[0]
    capacity = count // 2
    local = references.shape[0]
    width = references.shape[1]
    listed_count = candidates.shape[1]
    block_width = width // ROT
    row_count = groups * capacity
    listed_owner = candidates // local
    group_index = jnp.arange(groups, dtype=jnp.int32)
    present = jnp.any(listed_owner[:, :, None] == group_index[None, None, :], axis=1)
    ranking = jnp.cumsum(present.astype(jnp.int32), axis=0) - 1
    slot_index = jnp.arange(capacity, dtype=jnp.int32)
    class_assignment = present.T[:, None, :] & (ranking.T[:, None, :] == slot_index[None, :, None])
    outgoing = jnp.einsum(
        "evd,do->evo",
        class_assignment.astype(jnp.bfloat16),
        particles,
        preferred_element_type=jnp.float32,
    ).astype(jnp.bfloat16)
    particle_index = jnp.arange(count, dtype=jnp.int32)
    particle_records = jnp.concatenate(
        [
            candidates.astype(jnp.float32),
            offsets.astype(jnp.float32),
            particle_index[:, None].astype(jnp.float32),
            jnp.ones((count, 1), jnp.float32),
            jnp.zeros((count, 4), jnp.float32),
        ],
        axis=1,
    )
    meta_out = jnp.einsum(
        "yhu,um->yhm",
        class_assignment.astype(jnp.float32),
        particle_records,
        precision=lax.Precision.HIGHEST,
    ).astype(jnp.bfloat16)
    arrived, arrived_meta = (
        lax.all_to_all(outgoing, "cls", split_axis=0, concat_axis=0, tiled=True),
        lax.all_to_all(meta_out, "cls", split_axis=0, concat_axis=0, tiled=True),
    )
    details = arrived_meta.astype(jnp.float32).reshape(row_count, -1)
    listed = details[:, :listed_count].astype(jnp.int32)
    prior_x = details[:, listed_count].astype(jnp.int32)
    prior_y = details[:, listed_count + 1].astype(jnp.int32)
    filled = details[:, listed_count + 3] > 0.5
    class_index = owner * local + jnp.arange(local, dtype=jnp.int32)
    allowed = jnp.any(listed[:, :, None] == class_index[None, None, :], axis=1) & filled[:, None]
    turn_index = jnp.arange(ROT, dtype=jnp.int32)
    diagonal = (
        turn_index[None, :, None] == (turn_index[:, None, None] - turn_index[None, None, :]) % ROT
    )
    diagonal_f32 = diagonal.astype(jnp.float32)
    diagonal_bf16 = diagonal.astype(jnp.bfloat16)
    class_refs = references.reshape(local, ROT, block_width)
    images = arrived.reshape(row_count, ANGLES, 2, CYCLES)
    moved_list = []
    score_list = []
    for shift in range(SHIFTS):
        phase = phase_angles(prior_x + SHIFT_X_STEPS[shift], prior_y + SHIFT_Y_STEPS[shift])
        moved = shift_images(images, phase).reshape(row_count, ROT, block_width)
        pairs = jnp.einsum("xjf,clf->xjcl", moved, class_refs, preferred_element_type=jnp.float32)
        score_values = SOFTMAX_WARMTH * jnp.einsum(
            "xjcl,jlr->xcr", pairs, diagonal_f32, precision=lax.Precision.HIGHEST
        )
        moved_list.append(moved)
        score_list.append(score_values)
    all_scores = jnp.stack(score_list, axis=1)
    allowed_wide = allowed[:, None, :, None]
    local_max = jnp.max(jnp.where(allowed_wide, all_scores, NEGATIVE), axis=(1, 2, 3))
    local_sum = jnp.sum(
        jnp.exp(jnp.where(allowed_wide, all_scores - local_max[:, None, None, None], NEGATIVE)),
        axis=(1, 2, 3),
    )
    back_max, back_sum = (
        lax.all_to_all(
            local_max.reshape(groups, capacity), "cls", split_axis=0, concat_axis=0, tiled=True
        ),
        lax.all_to_all(
            local_sum.reshape(groups, capacity), "cls", split_axis=0, concat_axis=0, tiled=True
        ),
    )
    owner_max = jnp.max(jnp.where(class_assignment, back_max[:, :, None], NEGATIVE), axis=1)
    owner_sum = jnp.sum(jnp.where(class_assignment, back_sum[:, :, None], 0.0), axis=1)
    whole_max = jnp.max(owner_max, axis=0)
    whole_sum = jnp.sum(owner_sum * jnp.exp(owner_max - whole_max[None, :]), axis=0)
    slot_max = jnp.sum(jnp.where(class_assignment, whole_max[None, None, :], 0.0), axis=2)
    slot_sum = jnp.sum(jnp.where(class_assignment, whole_sum[None, None, :], 0.0), axis=2)
    total_max, total_sum = (
        lax.all_to_all(slot_max, "cls", split_axis=0, concat_axis=0, tiled=True),
        lax.all_to_all(slot_sum, "cls", split_axis=0, concat_axis=0, tiled=True),
    )
    total_max = total_max.reshape(row_count)
    total_sum = total_sum.reshape(row_count)
    safe_sum = jnp.where(filled, total_sum, 1.0)
    totals = jnp.zeros((local, ROT, block_width), jnp.float32)
    masses = jnp.zeros((local,), jnp.float32)
    for shift in range(SHIFTS):
        exponent = jnp.exp(
            jnp.where(allowed[:, :, None], score_list[shift] - total_max[:, None, None], NEGATIVE)
        )
        weight = (exponent / safe_sum[:, None, None]).astype(jnp.bfloat16)
        masses = masses + jnp.sum(weight.astype(jnp.float32), axis=(0, 2))
        spread = jnp.einsum(
            "xcr,jlr->xcjl", weight, diagonal_bf16, preferred_element_type=jnp.float32
        ).astype(jnp.bfloat16)
        totals = totals + jnp.einsum(
            "xcjl,xjf->clf", spread, moved_list[shift], preferred_element_type=jnp.float32
        )
    return unpack_average(reduce_average(pack_payload(totals, masses)))


def solution(mesh):
    in_specs = (
        P(("cls", "dom"), None),
        P("cls", None),
        P(("cls", "dom"), None),
        P(("cls", "dom"), None),
    )
    out_specs = P("cls", None)
    return jax.shard_map(shards, mesh=mesh, in_specs=in_specs, out_specs=out_specs, check_vma=False)
```

```python
import math
import numpy as np
import jax, jax.numpy as jnp
from jax import lax
from jax.experimental import pallas as pl
from jax.experimental.pallas import tpu as pltpu
from jax.sharding import PartitionSpec as P

MESH = pl.DeviceIdType.MESH
CYCLES, ANGLES, ROTS, SHIFTS, BOX = 128, 144, 36, 5, 256
CLS_LOC, NCH, RC, LEAD, DROWS = 25, 3, 80, 15, 225
GROUPS, SLOTS, PART = 8, 16, 4
NEGATIVE = -1e30
WIDTH, LHS_ROWS, ACC_ROWS = 1024, 48, 40


def unit_tables():
    angle = 2.0 * math.pi * np.arange(ANGLES) / ANGLES
    radius = np.arange(1, CYCLES + 1)
    out = np.zeros((2, 2, 4, ACC_ROWS, CYCLES), np.float64)
    for axis, along in enumerate((np.cos(angle), np.sin(angle))):
        phase = (2.0 * math.pi / BOX) * along[:, None] * radius
        for part, value in enumerate((np.cos(phase), np.sin(phase))):
            out[axis, part, :, :ROTS] = value.reshape(ROTS, 4, CYCLES).transpose(1, 0, 2)
    return out.astype(np.float32)


def gather_kernel(p_ref, meta_ref, out_ref, mout_ref, lsem, ssem, rsem):
    me = lax.axis_index("cls")
    core = me % 2
    right, left, across = (me + 2) % GROUPS, (me + 6) % GROUPS, (me + 4) % GROUPS
    pair = me + 1 - 2 * core
    shift = pair - me
    barrier = pltpu.get_barrier_semaphore()
    for k in range(1, GROUPS):
        pl.semaphore_signal(barrier, inc=1, device_id={"cls": (me + k) % GROUPS}, device_id_type=MESH)
    pl.semaphore_wait(barrier, GROUPS - 1)
    h0, h1 = pl.ds(0, 2), pl.ds(2, 2)
    sends = []

    def send(src, dst, i, target):
        copy = pltpu.make_async_remote_copy(src_ref=src, dst_ref=dst, send_sem=ssem.at[i], recv_sem=rsem.at[i],
                                            device_id={"cls": target}, device_id_type=MESH)
        copy.start()
        sends.append(copy)
        return copy

    metas = [send(meta_ref, mout_ref.at[me], 13 + k, (me + k) % GROUPS) for k in range(1, GROUPS)]
    r0 = send(p_ref.at[h0], out_ref.at[me, h0], 0, right)
    l1 = send(p_ref.at[h1], out_ref.at[me, h1], 1, left)
    r1 = send(p_ref.at[h1], out_ref.at[me, h1], 2, right)
    l0 = send(p_ref.at[h0], out_ref.at[me, h0], 3, left)
    own = send(p_ref, out_ref.at[me], 4, pair)
    local = pltpu.make_async_copy(p_ref, out_ref.at[me], lsem.at[0])
    local.start()
    mlocal = pltpu.make_async_copy(meta_ref, mout_ref.at[me], lsem.at[1])
    mlocal.start()
    r0.wait_recv()
    fr = send(out_ref.at[left, h0], out_ref.at[left, h0], 5, right)
    s0 = send(out_ref.at[left, h0], out_ref.at[left, h0], 7, pair)
    l1.wait_recv()
    fl = send(out_ref.at[right, h1], out_ref.at[right, h1], 6, left)
    s1 = send(out_ref.at[right, h1], out_ref.at[right, h1], 8, pair)
    r1.wait_recv()
    s2 = send(out_ref.at[left, h1], out_ref.at[left, h1], 9, pair)
    l0.wait_recv()
    s3 = send(out_ref.at[right, h0], out_ref.at[right, h0], 10, pair)
    fr.wait_recv()
    s4 = send(out_ref.at[across, h0], out_ref.at[across, h0], 11, pair)
    fl.wait_recv()
    s5 = send(out_ref.at[across, h1], out_ref.at[across, h1], 12, pair)
    for copy in [own, s0, s1, s2, s3, s4, s5] + metas:
        copy.wait_recv()
    local.wait()
    mlocal.wait()
    for copy in sends:
        copy.wait_send()


def gather_particles(images, meta):
    vmem = pl.BlockSpec(memory_space=pltpu.VMEM)
    return pl.pallas_call(
        gather_kernel,
        out_shape=(jax.ShapeDtypeStruct((GROUPS, PART, 288, 128), jnp.bfloat16),
                   jax.ShapeDtypeStruct((GROUPS, 8, 128), jnp.int32)),
        in_specs=[vmem, vmem],
        out_specs=(vmem, vmem),
        scratch_shapes=[pltpu.SemaphoreType.DMA((2,)), pltpu.SemaphoreType.DMA((21,)), pltpu.SemaphoreType.DMA((21,))],
        compiler_params=pltpu.CompilerParams(collective_id=1, has_side_effects=True, vmem_limit_bytes=16 << 20),
        name="gather_particles",
    )(images, meta)


def group_turn(lane):
    return lane - jnp.where(lane >= 80, 80, jnp.where(lane >= 40, 40, 0))


def lane_places(rows):
    row = lax.broadcasted_iota(jnp.int32, (rows, 128), 0)
    lane = lax.broadcasted_iota(jnp.int32, (rows, 128), 1)
    return row, lane, group_turn(lane)


def score_kernel(meta, unit, images, refs, scores, moved, stats, table, wide, powers):
    slot = pl.program_id(0)
    owner = lax.axis_index("cls")

    @pl.when(slot == 0)
    def _():
        for v in range(GROUPS):
            table[2 * v * 8 + 5] = 0
            table[(2 * v + 1) * 8 + 5] = 0
            place = jnp.int32(2 * v)
            for i in range(PART):
                k = jnp.int32(0)
                for t in range(8):
                    c = meta[v, i, t] - owner * CLS_LOC
                    table[place * 8 + k] = c
                    k = k + jnp.where((c >= 0) & (c < CLS_LOC), 1, 0)
                hit = jnp.where(k > 0, 1, 0)

                @pl.when(hit > 0)
                def _():
                    table[place * 8 + 5] = 1
                    table[place * 8 + 6] = PART * v + i

                place = place + hit
        wide[288:320, :] = jnp.zeros((32, 128), jnp.float32)
        for axis in range(2):
            powers[axis, 0, 0] = jnp.ones((4, ACC_ROWS, 128), jnp.float32)
            powers[axis, 0, 1] = jnp.zeros((4, ACC_ROWS, 128), jnp.float32)
            powers[axis, 1] = unit[axis]
            for t in range(2, 8):
                c0, s0 = powers[axis, t - 1, 0], powers[axis, t - 1, 1]
                c1, s1 = unit[axis, 0], unit[axis, 1]
                powers[axis, t, 0] = c0 * c1 - s0 * s1
                powers[axis, t, 1] = s0 * c1 + c0 * s1
        stats[0] = jnp.full((GROUPS * PART, 128), NEGATIVE, jnp.float32)
        stats[1] = jnp.zeros((GROUPS * PART, 128), jnp.float32)

    @pl.when(table[slot * 8 + 5] > 0)
    def _():
        pid = table[slot * 8 + 6]
        v, i = pid // PART, pid % PART
        tx, ty = meta[v, i, 8], meta[v, i, 9]
        ax, ay = jnp.abs(tx), jnp.abs(ty)
        gx = jnp.where(tx < 0, -1.0, 1.0).astype(jnp.float32)
        gy = jnp.where(ty < 0, -1.0, 1.0).astype(jnp.float32)
        wide[0:288, :] = images[v, i].astype(jnp.float32)
        gap8, gap48 = jnp.zeros((8, 128), jnp.float32), jnp.zeros((48, 128), jnp.float32)
        for a in range(4):
            re = wide[pl.ds(2 * a, ACC_ROWS, stride=8), :]
            im = wide[pl.ds(2 * a + 1, ACC_ROWS, stride=8), :]
            cx, sx = powers[0, ax, 0, a], powers[0, ax, 1, a] * gx
            cy, sy = powers[1, ay, 0, a], powers[1, ay, 1, a] * gy
            bc, bs = cx * cy - sx * sy, sx * cy + cx * sy
            zr, zi = re * bc + im * bs, im * bc - re * bs
            real, imag = [zr], [zi]
            for axis in range(2):
                uc, us = unit[axis, 0, a], unit[axis, 1, a]
                rc, rs, ic, js = zr * uc, zr * us, zi * uc, zi * us
                real += [rc + js, rc - js]
                imag += [ic - rs, ic + rs]
            for m, part in enumerate((real, imag)):
                lanes = pl.ds(256 * a + 128 * m, 128)
                moved[0, 0:128, lanes] = jnp.concatenate(part[0:3] + [gap8], axis=0).astype(jnp.bfloat16)
                moved[0, 128:256, lanes] = jnp.concatenate(part[3:5] + [gap48], axis=0).astype(jnp.bfloat16)
        lhs = jnp.concatenate([refs[table[slot * 8 + k]] for k in range(4)], axis=0)
        pairs = lax.dot_general(lhs, moved[0], (((1,), (1,)), ((), ())), preferred_element_type=jnp.float32)
        row = lax.broadcasted_iota(jnp.int32, (ACC_ROWS, 128), 0)
        lane = lax.broadcasted_iota(jnp.int32, (ACC_ROWS, 128), 1)
        turn = group_turn(jnp.where(lane >= ROTS - 1, lane - (ROTS - 1), lane + 128 - (ROTS - 1)))
        turn2 = group_turn(jnp.where(lane == 127, 0, lane + 1))
        back = (ROTS - 1) - row
        direct = (turn + back < ROTS) & (back >= 0)
        wrapped = (turn2 < ROTS) & (turn2 + back >= ROTS)
        _, lane1, turn1 = lane_places(8)
        lines = []
        for half in range(2):
            rows = []
            for k in range(4):
                block = pairs[LHS_ROWS * k:LHS_ROWS * k + ACC_ROWS, 128 * half:128 * half + 128]
                skew = pltpu.roll(block, 0, 1, stride=1, stride_axis=0)
                near = jnp.sum(jnp.where(direct, skew, 0.0), axis=0, keepdims=True)
                far = jnp.sum(jnp.where(wrapped, skew, 0.0), axis=0, keepdims=True)
                rows.append((near, far))
            near = jnp.concatenate([r[0] for r in rows] + [jnp.zeros((4, 128), jnp.float32)], axis=0)
            far = jnp.concatenate([r[1] for r in rows] + [jnp.zeros((4, 128), jnp.float32)], axis=0)
            whole = 2.0 * (pltpu.roll(near, 128 - (ROTS - 1), 1) + pltpu.roll(far, 1, 1))
            row8 = lax.broadcasted_iota(jnp.int32, (8, 128), 0)
            good = (turn1 < ROTS) & (lane1 < (120 if half == 0 else 80)) & (row8 < 4)
            line = jnp.where(good, whole, NEGATIVE)
            scores[0, :, 128 * half:128 * half + 128] = line
            lines.append(line)
        best = jnp.max(jnp.max(jnp.maximum(lines[0], lines[1]), axis=1, keepdims=True), axis=0, keepdims=True)
        power = jnp.exp(lines[0] - best) + jnp.exp(lines[1] - best)
        mass = jnp.sum(jnp.sum(power, axis=1, keepdims=True), axis=0, keepdims=True)
        stats[0, pl.ds(pid, 1), :] = jnp.broadcast_to(best, (1, 128))
        stats[1, pl.ds(pid, 1), :] = jnp.broadcast_to(mass, (1, 128))


def score_slots(meta, unit, images, refs):
    vmem, smem = pl.BlockSpec(memory_space=pltpu.VMEM), pl.BlockSpec(memory_space=pltpu.SMEM)
    return pl.pallas_call(
        score_kernel,
        grid=(SLOTS,),
        out_shape=(jax.ShapeDtypeStruct((SLOTS, 8, 256), jnp.float32),
                   jax.ShapeDtypeStruct((SLOTS, 256, WIDTH), jnp.bfloat16),
                   jax.ShapeDtypeStruct((2, GROUPS * PART, 128), jnp.float32),
                   jax.ShapeDtypeStruct((17 * 8,), jnp.int32)),
        in_specs=[smem, vmem, vmem, vmem],
        out_specs=(pl.BlockSpec((1, 8, 256), lambda i: (i, 0, 0)),
                   pl.BlockSpec((1, 256, WIDTH), lambda i: (i, 0, 0)), vmem, smem),
        scratch_shapes=[pltpu.VMEM((320, 128), jnp.float32),
                        pltpu.VMEM((2, 8, 2, 4, ACC_ROWS, 128), jnp.float32)],
        compiler_params=pltpu.CompilerParams(vmem_limit_bytes=40 << 20),
        name="score_slots",
    )(meta, unit, images, refs)


def norm_kernel(stats, total, boxes, ssem, rsem):
    me = lax.axis_index("cls")
    barrier = pltpu.get_barrier_semaphore()
    for k in range(1, GROUPS):
        pl.semaphore_signal(barrier, inc=1, device_id={"cls": (me + k) % GROUPS}, device_id_type=MESH)
    pl.semaphore_wait(barrier, GROUPS - 1)
    copies = []
    for k in range(1, GROUPS):
        copy = pltpu.make_async_remote_copy(src_ref=stats, dst_ref=boxes.at[k - 1], send_sem=ssem.at[k - 1],
                                            recv_sem=rsem.at[k - 1], device_id={"cls": (me + k) % GROUPS},
                                            device_id_type=MESH)
        copy.start()
        copies.append(copy)
    for copy in copies:
        copy.wait_recv()
    best = stats[0]
    for k in range(GROUPS - 1):
        best = jnp.maximum(best, boxes[k, 0])
    whole = stats[1] * jnp.exp(stats[0] - best)
    for k in range(GROUPS - 1):
        whole = whole + boxes[k, 1] * jnp.exp(boxes[k, 0] - best)
    total[0] = best
    total[1] = whole
    for copy in copies:
        copy.wait_send()


def normalise(stats):
    vmem = pl.BlockSpec(memory_space=pltpu.VMEM)
    return pl.pallas_call(
        norm_kernel,
        out_shape=jax.ShapeDtypeStruct((2, GROUPS * PART, 128), jnp.float32),
        in_specs=[vmem],
        out_specs=vmem,
        scratch_shapes=[pltpu.VMEM((GROUPS - 1, 2, GROUPS * PART, 128), jnp.float32),
                        pltpu.SemaphoreType.DMA((7,)), pltpu.SemaphoreType.DMA((7,))],
        compiler_params=pltpu.CompilerParams(collective_id=2, has_side_effects=True),
        name="normalise",
    )(stats)


def sum_kernel(table, total, scores, moved, out, acc, comp, masses):
    slot = pl.program_id(0)

    @pl.when(slot == 0)
    def _():
        acc[...] = jnp.zeros(acc.shape, jnp.float32)
        masses[...] = jnp.zeros(masses.shape, jnp.float32)

    @pl.when(table[slot * 8 + 5] > 0)
    def _():
        pid = table[slot * 8 + 6]
        best, whole = total[0, pl.ds(pid, 1), :], total[1, pl.ds(pid, 1), :]
        row, _, turn = lane_places(ACC_ROWS)
        later = turn >= row
        halves = []
        mass = jnp.zeros((8, 1), jnp.float32)
        for half in range(2):
            weight = jnp.exp(scores[0, :, 128 * half:128 * half + 128] - best) / whole
            weight = weight.astype(jnp.bfloat16).astype(jnp.float32)
            mass = mass + jnp.sum(weight, axis=1, keepdims=True)
            back = pltpu.roll(weight, 92, 1)
            rows = []
            for k in range(4):
                one = jnp.broadcast_to(weight[k:k + 1, :], (ACC_ROWS, 128))
                two = jnp.broadcast_to(back[k:k + 1, :], (ACC_ROWS, 128))
                rows.append(jnp.where(later, pltpu.roll(one, 0, 1, stride=1, stride_axis=0),
                                      pltpu.roll(two, 0, 1, stride=1, stride_axis=0)))
            halves.append(jnp.concatenate(rows, axis=0))
        spread = jnp.concatenate(halves, axis=1).astype(jnp.bfloat16)
        for k in range(4):
            c = table[slot * 8 + k]
            masses[pl.ds(c, 1), :] = masses[pl.ds(c, 1), :] + jnp.broadcast_to(mass[k:k + 1, :], (1, 128))
        contrib = jnp.dot(spread, moved[0], preferred_element_type=jnp.float32)
        for k in range(4):
            c = table[slot * 8 + k]
            acc[c] = acc[c] + contrib[ACC_ROWS * k:ACC_ROWS * (k + 1)]

    @pl.when(slot == SLOTS - 1)
    def _():
        row = lax.broadcasted_iota(jnp.int32, (32, 128), 0)
        lane = lax.broadcasted_iota(jnp.int32, (32, 128), 1)
        line = jnp.sum(jnp.where(row == lane, masses[...], 0.0), axis=0, keepdims=True)
        high = line.astype(jnp.bfloat16).astype(jnp.float32)
        lead = jnp.concatenate([high, line - high, jnp.zeros((14, 128), jnp.float32)], axis=0)
        for y in range(4):
            comp[y * 240:y * 240 + 16, :] = jnp.concatenate([lead] * 8, axis=1)
        for c in range(CLS_LOC):
            start = c * ROTS
            while start < (c + 1) * ROTS:
                y = start // DROWS
                stop = min((c + 1) * ROTS, (y + 1) * DROWS)
                to = y * 240 + LEAD + start - y * DROWS
                comp[to:to + stop - start, :] = acc[c, start - c * ROTS:stop - c * ROTS, :]
                start = stop
        for ch in range(NCH):
            for y in range(4):
                for z in range(8):
                    out[ch, y, z] = comp[y * 240 + ch * RC:y * 240 + (ch + 1) * RC,
                                         128 * z:128 * z + 128].astype(jnp.bfloat16)


def sum_slots(table, total, scores, moved):
    vmem, smem = pl.BlockSpec(memory_space=pltpu.VMEM), pl.BlockSpec(memory_space=pltpu.SMEM)
    return pl.pallas_call(
        sum_kernel,
        grid=(SLOTS,),
        out_shape=jax.ShapeDtypeStruct((NCH, 4, 8, RC, 128), jnp.bfloat16),
        in_specs=[smem, vmem, pl.BlockSpec((1, 8, 256), lambda i: (i, 0, 0)),
                  pl.BlockSpec((1, 256, WIDTH), lambda i: (i, 0, 0))],
        out_specs=vmem,
        scratch_shapes=[pltpu.VMEM((CLS_LOC, ACC_ROWS, WIDTH), jnp.float32),
                        pltpu.VMEM((960, WIDTH), jnp.float32),
                        pltpu.VMEM((32, 128), jnp.float32)],
        compiler_params=pltpu.CompilerParams(vmem_limit_bytes=40 << 20),
        name="sum_slots",
    )(table, total, scores, moved)


def reduce_kernel(p_ref, g_ref, x1, x2, d3, d4, e5, e6, c1, c2, s_buf, z_buf, ysend, yrecv, zsend, zrecv):
    dom = lax.axis_index("dom")
    y = dom % 4
    z = dom // 4
    yp, ym, yo = (y + 1) % 4, (y + 3) % 4, (y + 2) % 4
    up, down = {"dom": z * 4 + yp}, {"dom": z * 4 + ym}
    zdev = [{"dom": ((z + k) % 8) * 4 + y} for k in range(8)]
    barrier = pltpu.get_barrier_semaphore()
    for target in [up, down] + zdev[1:]:
        pl.semaphore_signal(barrier, inc=1, device_id=target, device_id_type=MESH)
    pl.semaphore_wait(barrier, 9)
    A, B = pl.ds(0, 4), pl.ds(4, 4)

    def send(src, dst, ssem, rsem, target):
        copy = pltpu.make_async_remote_copy(src_ref=src, dst_ref=dst, send_sem=ssem, recv_sem=rsem,
                                            device_id=target, device_id_type=MESH)
        copy.start()
        return copy

    pending = []
    m1, m2, m3, m4, m5, m6 = {}, {}, {}, {}, {}, {}
    for ch in range(NCH):
        m1[ch] = send(p_ref.at[ch, yo, A], x1.at[ch], ysend.at[ch, 0], yrecv.at[ch, 0], up)
        m2[ch] = send(p_ref.at[ch, yo, B], x2.at[ch], ysend.at[ch, 1], yrecv.at[ch, 1], down)
        m3[ch] = send(p_ref.at[ch, yp, B], d3.at[ch], ysend.at[ch, 2], yrecv.at[ch, 2], up)
        m4[ch] = send(p_ref.at[ch, ym, A], d4.at[ch], ysend.at[ch, 3], yrecv.at[ch, 3], down)
    for ch in range(NCH):
        m1[ch].wait_recv()
        c1[ch] = (x1[ch].astype(jnp.float32) + p_ref[ch, yp, A].astype(jnp.float32)).astype(jnp.bfloat16)
        m5[ch] = send(c1.at[ch], e5.at[ch], ysend.at[ch, 4], yrecv.at[ch, 4], up)
        m2[ch].wait_recv()
        c2[ch] = (x2[ch].astype(jnp.float32) + p_ref[ch, ym, B].astype(jnp.float32)).astype(jnp.bfloat16)
        m6[ch] = send(c2.at[ch], e6.at[ch], ysend.at[ch, 5], yrecv.at[ch, 5], down)
    zm = {}
    for ch in range(NCH):
        m4[ch].wait_recv()
        m5[ch].wait_recv()
        s_buf[ch, A] = (p_ref[ch, y, A].astype(jnp.float32) + e5[ch].astype(jnp.float32)
                        + d4[ch].astype(jnp.float32)).astype(jnp.bfloat16)
        m3[ch].wait_recv()
        m6[ch].wait_recv()
        s_buf[ch, B] = (p_ref[ch, y, B].astype(jnp.float32) + e6[ch].astype(jnp.float32)
                        + d3[ch].astype(jnp.float32)).astype(jnp.bfloat16)
        for k in range(1, 8):
            zm[ch, k] = send(s_buf.at[ch, (z + k) % 8], z_buf.at[ch, k - 1],
                             zsend.at[ch, k - 1], zrecv.at[ch, k - 1], zdev[k])
    zg = {}
    mass = None
    for ch in range(NCH):
        num = s_buf[ch, z].astype(jnp.float32)
        for k in range(1, 8):
            zm[ch, k].wait_recv()
            num = num + z_buf[ch, k - 1].astype(jnp.float32)
        if ch == 0:
            mass = num[0:1, :] + num[1:2, :] + 1.0
        place = DROWS * y + (ch * RC - LEAD) + lax.broadcasted_iota(jnp.int32, (RC, 128), 0)
        den = jnp.ones((RC, 128), jnp.float32)
        for c in range(CLS_LOC):
            here = (place >= c * ROTS) & (place < (c + 1) * ROTS)
            den = jnp.where(here, jnp.broadcast_to(mass[:, c:c + 1], (RC, 128)), den)
        g_ref[ch, y, z] = (num / den).astype(jnp.bfloat16)
        for k in range(1, 8):
            zg[ch, k] = send(g_ref.at[ch, y, z], g_ref.at[ch, y, z],
                             zsend.at[ch, 6 + k], zrecv.at[ch, 6 + k], zdev[k])
    m7, m8, m9, m10 = {}, {}, {}, {}
    for ch in range(NCH):
        for k in range(1, 8):
            zg[ch, k].wait_recv()
        m7[ch] = send(g_ref.at[ch, y], g_ref.at[ch, y], ysend.at[ch, 6], yrecv.at[ch, 6], up)
        m8[ch] = send(g_ref.at[ch, y], g_ref.at[ch, y], ysend.at[ch, 7], yrecv.at[ch, 7], down)
    for ch in range(NCH):
        m7[ch].wait_recv()
        m9[ch] = send(g_ref.at[ch, ym, A], g_ref.at[ch, ym, A], ysend.at[ch, 8], yrecv.at[ch, 8], up)
        m8[ch].wait_recv()
        m10[ch] = send(g_ref.at[ch, yp, B], g_ref.at[ch, yp, B], ysend.at[ch, 9], yrecv.at[ch, 9], down)
    for ch in range(NCH):
        m9[ch].wait_recv()
        m10[ch].wait_recv()
    for group in (m1, m2, m3, m4, m5, m6, zm, zg, m7, m8, m9, m10):
        for copy in group.values():
            copy.wait_send()


def reduce_average(payload):
    half = pltpu.VMEM((NCH, 4, RC, 128), jnp.bfloat16)
    return pl.pallas_call(
        reduce_kernel,
        out_shape=jax.ShapeDtypeStruct((NCH, 4, 8, RC, 128), jnp.bfloat16),
        in_specs=[pl.BlockSpec(memory_space=pltpu.VMEM)],
        out_specs=pl.BlockSpec(memory_space=pltpu.VMEM),
        scratch_shapes=[half] * 8 + [
            pltpu.VMEM((NCH, 8, RC, 128), jnp.bfloat16),
            pltpu.VMEM((NCH, 7, RC, 128), jnp.bfloat16),
            pltpu.SemaphoreType.DMA((NCH, 10)),
            pltpu.SemaphoreType.DMA((NCH, 10)),
            pltpu.SemaphoreType.DMA((NCH, 14)),
            pltpu.SemaphoreType.DMA((NCH, 14)),
        ],
        compiler_params=pltpu.CompilerParams(collective_id=5, has_side_effects=True, vmem_limit_bytes=40 << 20),
        name="reduce_average",
    )(payload)


def unpack_average(gathered):
    rows = gathered.transpose(1, 0, 3, 2, 4).reshape(4, NCH * RC, 8, 128)[:, LEAD:]
    return rows.reshape(CLS_LOC, 36864)


def shards(particles, references, candidates, offsets):
    meta = jnp.pad(jnp.concatenate([candidates, offsets], axis=1), ((0, 4), (0, 118)))
    images, meta = gather_particles(particles.reshape(PART, 288, 128), meta)
    refs = jnp.pad(references.reshape(CLS_LOC, ROTS, WIDTH)[:, ::-1], ((0, 0), (0, LHS_ROWS - ROTS), (0, 0)))
    scores, moved, stats, table = score_slots(meta, jnp.asarray(unit_tables()), images, refs)
    payload = sum_slots(table, normalise(stats), scores, moved)
    return unpack_average(reduce_average(payload))


def solution(mesh):
    in_specs = (
        P(("cls", "dom"), None),
        P("cls", None),
        P(("cls", "dom"), None),
        P(("cls", "dom"), None),
    )
    return jax.shard_map(shards, mesh=mesh, in_specs=in_specs, out_specs=P("cls", None), check_vma=False)
```

```python
import math
import numpy as np
import jax, jax.numpy as jnp
from jax import lax
from jax.experimental import pallas as pl
from jax.experimental.pallas import tpu as pltpu
from jax.sharding import PartitionSpec as P

MESH = pl.DeviceIdType.MESH
CYCLES, ANGLES, ROTS, SHIFTS, BOX = 128, 144, 36, 5, 256
CLS_LOC, NCH, RC, LEAD, DROWS = 25, 5, 48, 15, 225
GROUPS, SLOTS, PART = 8, 16, 4
NEGATIVE = -1e30
WIDTH, LHS_ROWS, ACC_ROWS = 1024, 48, 40


def unit_tables():
    angle = 2.0 * math.pi * np.arange(ANGLES) / ANGLES
    radius = np.arange(1, CYCLES + 1)
    out = np.zeros((2, 2, 4, ACC_ROWS, CYCLES), np.float64)
    for axis, along in enumerate((np.cos(angle), np.sin(angle))):
        phase = (2.0 * math.pi / BOX) * along[:, None] * radius
        for part, value in enumerate((np.cos(phase), np.sin(phase))):
            out[axis, part, :, :ROTS] = value.reshape(ROTS, 4, CYCLES).transpose(1, 0, 2)
    return out.astype(np.float32)


def gather_kernel(p_ref, cand_ref, offs_ref, refs_ref, out_ref, cout_ref, oout_ref, rows_ref, tall, lsem, ssem, rsem):
    me = lax.axis_index("cls")
    core = me % 2
    right, left, across = (me + 2) % GROUPS, (me + 6) % GROUPS, (me + 4) % GROUPS
    pair = me + 1 - 2 * core
    shift = pair - me
    barrier = pltpu.get_barrier_semaphore()
    for k in range(1, GROUPS):
        pl.semaphore_signal(barrier, inc=1, device_id={"cls": (me + k) % GROUPS}, device_id_type=MESH)
    pl.semaphore_wait(barrier, GROUPS - 1)
    h0, h1 = pl.ds(0, 2), pl.ds(2, 2)
    sends = []

    def send(src, dst, i, target):
        copy = pltpu.make_async_remote_copy(src_ref=src, dst_ref=dst, send_sem=ssem.at[i], recv_sem=rsem.at[i],
                                            device_id={"cls": target}, device_id_type=MESH)
        copy.start()
        sends.append(copy)
        return copy

    metas = [send(cand_ref, cout_ref.at[me], 12 + k, (me + k) % GROUPS) for k in range(1, GROUPS)]
    metas += [send(offs_ref, oout_ref.at[me], 19 + k, (me + k) % GROUPS) for k in range(1, GROUPS)]
    r0 = send(p_ref.at[h0], out_ref.at[me, h0], 0, right)
    l1 = send(p_ref.at[h1], out_ref.at[me, h1], 1, left)
    r1 = send(p_ref.at[h1], out_ref.at[me, h1], 2, right)
    l0 = send(p_ref.at[h0], out_ref.at[me, h0], 3, left)
    own = send(p_ref, out_ref.at[me], 4, pair)
    locals_ = [pltpu.make_async_copy(p_ref, out_ref.at[me], lsem.at[0]),
               pltpu.make_async_copy(cand_ref, cout_ref.at[me], lsem.at[1]),
               pltpu.make_async_copy(offs_ref, oout_ref.at[me], lsem.at[2])]
    for copy in locals_:
        copy.start()

    def clear(c, carry):
        for g in range(8):
            tall[g, pl.ds(pl.multiple_of(c * LHS_ROWS + 32, 16), 16), :] = jnp.zeros((16, 128), jnp.float32)
        return carry

    def spread(l, carry):
        value = refs_ref[:, pl.ds(pl.multiple_of(l * WIDTH, WIDTH), WIDTH)].astype(jnp.float32)
        for g in range(8):
            tall[g, pl.ds(ROTS - 1 - l, CLS_LOC, stride=LHS_ROWS), :] = value[:, 128 * g:128 * g + 128]
        return carry

    def pack(c, carry):
        rows = pl.ds(pl.multiple_of(c * LHS_ROWS, LHS_ROWS), LHS_ROWS)
        for g in range(8):
            rows_ref[c, :, 128 * g:128 * g + 128] = tall[g, rows, :].astype(jnp.bfloat16)
        return carry

    lax.fori_loop(0, CLS_LOC, clear, 0)
    lax.fori_loop(0, ROTS, spread, 0)
    r0.wait_recv()
    fr = send(out_ref.at[left, h0], out_ref.at[left, h0], 5, right)
    s0 = send(out_ref.at[left, h0], out_ref.at[left, h0], 7, pair)
    l1.wait_recv()
    fl = send(out_ref.at[right, h1], out_ref.at[right, h1], 6, left)
    s1 = send(out_ref.at[right, h1], out_ref.at[right, h1], 8, pair)
    lax.fori_loop(0, CLS_LOC, pack, 0)
    r1.wait_recv()
    s2 = send(out_ref.at[left, h1], out_ref.at[left, h1], 9, pair)
    l0.wait_recv()
    s3 = send(out_ref.at[right, h0], out_ref.at[right, h0], 10, pair)
    fr.wait_recv()
    s4 = send(out_ref.at[across, h0], out_ref.at[across, h0], 11, pair)
    fl.wait_recv()
    s5 = send(out_ref.at[across, h1], out_ref.at[across, h1], 12, pair)
    for copy in [own, s0, s1, s2, s3, s4, s5] + metas:
        copy.wait_recv()
    for copy in locals_:
        copy.wait()
    for copy in sends:
        copy.wait_send()


def gather_particles(images, candidates, offsets, refs):
    vmem = pl.BlockSpec(memory_space=pltpu.VMEM)
    return pl.pallas_call(
        gather_kernel,
        out_shape=(jax.ShapeDtypeStruct((GROUPS, PART, 288, 128), jnp.bfloat16),
                   jax.ShapeDtypeStruct((GROUPS, PART, 8), jnp.int32),
                   jax.ShapeDtypeStruct((GROUPS, PART, 2), jnp.int32),
                   jax.ShapeDtypeStruct((CLS_LOC, LHS_ROWS, WIDTH), jnp.bfloat16)),
        in_specs=[vmem] * 4,
        out_specs=(vmem,) * 4,
        scratch_shapes=[pltpu.VMEM((8, CLS_LOC * LHS_ROWS, 128), jnp.float32), pltpu.SemaphoreType.DMA((3,)),
                        pltpu.SemaphoreType.DMA((27,)), pltpu.SemaphoreType.DMA((27,))],
        compiler_params=pltpu.CompilerParams(collective_id=1, has_side_effects=True, vmem_limit_bytes=24 << 20),
        name="gather_particles",
    )(images, candidates, offsets, refs)


def group_turn(lane):
    return lane - jnp.where(lane >= 80, 80, jnp.where(lane >= 40, 40, 0))


def lane_places(rows):
    row = lax.broadcasted_iota(jnp.int32, (rows, 128), 0)
    lane = lax.broadcasted_iota(jnp.int32, (rows, 128), 1)
    return row, lane, group_turn(lane)


def score_kernel(cands, priors, unit, images, refs, scores, moved, stats, table, wide, powers):
    slot = pl.program_id(0)
    owner = lax.axis_index("cls")

    @pl.when(slot == 0)
    def _():
        for v in range(GROUPS):
            table[2 * v * 8 + 5] = 0
            table[(2 * v + 1) * 8 + 5] = 0
            place = jnp.int32(2 * v)
            for i in range(PART):
                k = jnp.int32(0)
                for t in range(8):
                    c = cands[v, i, t] - owner * CLS_LOC
                    table[place * 8 + k] = c
                    k = k + jnp.where((c >= 0) & (c < CLS_LOC), 1, 0)
                hit = jnp.where(k > 0, 1, 0)

                @pl.when(hit > 0)
                def _():
                    table[place * 8 + 5] = 1
                    table[place * 8 + 6] = PART * v + i

                place = place + hit
        wide[288:320, :] = jnp.zeros((32, 128), jnp.float32)
        for axis in range(2):
            powers[axis, 0, 0] = jnp.ones((4, ACC_ROWS, 128), jnp.float32)
            powers[axis, 0, 1] = jnp.zeros((4, ACC_ROWS, 128), jnp.float32)
            powers[axis, 1] = unit[axis]
            for t in range(2, 8):
                c0, s0 = powers[axis, t - 1, 0], powers[axis, t - 1, 1]
                c1, s1 = unit[axis, 0], unit[axis, 1]
                powers[axis, t, 0] = c0 * c1 - s0 * s1
                powers[axis, t, 1] = s0 * c1 + c0 * s1
        first = lax.broadcasted_iota(jnp.int32, (8, 128), 0) == 0
        stats[...] = jnp.where(first, NEGATIVE, 0.0)

    @pl.when(table[slot * 8 + 5] > 0)
    def _():
        pid = table[slot * 8 + 6]
        v, i = pid // PART, pid % PART
        tx, ty = priors[v, i, 0], priors[v, i, 1]
        ax, ay = jnp.abs(tx), jnp.abs(ty)
        gx = jnp.where(tx < 0, -1.0, 1.0).astype(jnp.float32)
        gy = jnp.where(ty < 0, -1.0, 1.0).astype(jnp.float32)
        wide[0:288, :] = images[v, i].astype(jnp.float32)
        gap8, gap48 = jnp.zeros((8, 128), jnp.float32), jnp.zeros((48, 128), jnp.float32)
        for a in range(4):
            re = wide[pl.ds(2 * a, ACC_ROWS, stride=8), :]
            im = wide[pl.ds(2 * a + 1, ACC_ROWS, stride=8), :]
            cx, sx = powers[0, ax, 0, a], powers[0, ax, 1, a] * gx
            cy, sy = powers[1, ay, 0, a], powers[1, ay, 1, a] * gy
            bc, bs = cx * cy - sx * sy, sx * cy + cx * sy
            zr, zi = re * bc + im * bs, im * bc - re * bs
            real, imag = [zr], [zi]
            for axis in range(2):
                uc, us = unit[axis, 0, a], unit[axis, 1, a]
                rc, rs, ic, js = zr * uc, zr * us, zi * uc, zi * us
                real += [rc + js, rc - js]
                imag += [ic - rs, ic + rs]
            for m, part in enumerate((real, imag)):
                lanes = pl.ds(256 * a + 128 * m, 128)
                moved[0, 0:128, lanes] = jnp.concatenate(part[0:3] + [gap8], axis=0).astype(jnp.bfloat16)
                moved[0, 128:256, lanes] = jnp.concatenate(part[3:5] + [gap48], axis=0).astype(jnp.bfloat16)
        lhs = jnp.concatenate([refs[table[slot * 8 + k]] for k in range(4)], axis=0)
        pairs = lax.dot_general(lhs, moved[0], (((1,), (1,)), ((), ())), preferred_element_type=jnp.float32)
        row = lax.broadcasted_iota(jnp.int32, (ACC_ROWS, 128), 0)
        lane = lax.broadcasted_iota(jnp.int32, (ACC_ROWS, 128), 1)
        turn = group_turn(jnp.where(lane >= ROTS - 1, lane - (ROTS - 1), lane + 128 - (ROTS - 1)))
        turn2 = group_turn(jnp.where(lane == 127, 0, lane + 1))
        back = (ROTS - 1) - row
        direct = (turn + back < ROTS) & (back >= 0)
        wrapped = (turn2 < ROTS) & (turn2 + back >= ROTS)
        _, lane1, turn1 = lane_places(8)
        lines = []
        for half in range(2):
            rows = []
            for k in range(4):
                block = pairs[LHS_ROWS * k:LHS_ROWS * k + ACC_ROWS, 128 * half:128 * half + 128]
                skew = pltpu.roll(block, 0, 1, stride=1, stride_axis=0)
                near = jnp.sum(jnp.where(direct, skew, 0.0), axis=0, keepdims=True)
                far = jnp.sum(jnp.where(wrapped, skew, 0.0), axis=0, keepdims=True)
                rows.append((near, far))
            near = jnp.concatenate([r[0] for r in rows] + [jnp.zeros((4, 128), jnp.float32)], axis=0)
            far = jnp.concatenate([r[1] for r in rows] + [jnp.zeros((4, 128), jnp.float32)], axis=0)
            whole = 2.0 * (pltpu.roll(near, 128 - (ROTS - 1), 1) + pltpu.roll(far, 1, 1))
            row8 = lax.broadcasted_iota(jnp.int32, (8, 128), 0)
            good = (turn1 < ROTS) & (lane1 < (120 if half == 0 else 80)) & (row8 < 4)
            line = jnp.where(good, whole, NEGATIVE)
            scores[0, :, 128 * half:128 * half + 128] = line
            lines.append(line)
        best = jnp.max(jnp.max(jnp.maximum(lines[0], lines[1]), axis=1, keepdims=True), axis=0, keepdims=True)
        power = jnp.exp(lines[0] - best) + jnp.exp(lines[1] - best)
        mass = jnp.sum(jnp.sum(power, axis=1, keepdims=True), axis=0, keepdims=True)
        place = lax.broadcasted_iota(jnp.int32, (1, 128), 1) == pid
        stats[0:1, :] = jnp.where(place, best, stats[0:1, :])
        stats[1:2, :] = jnp.where(place, mass, stats[1:2, :])


def score_slots(cands, priors, unit, images, refs):
    vmem, smem = pl.BlockSpec(memory_space=pltpu.VMEM), pl.BlockSpec(memory_space=pltpu.SMEM)
    return pl.pallas_call(
        score_kernel,
        grid=(SLOTS,),
        out_shape=(jax.ShapeDtypeStruct((SLOTS, 8, 256), jnp.float32),
                   jax.ShapeDtypeStruct((SLOTS, 256, WIDTH), jnp.bfloat16),
                   jax.ShapeDtypeStruct((8, 128), jnp.float32),
                   jax.ShapeDtypeStruct((17 * 8,), jnp.int32)),
        in_specs=[smem, smem, vmem, vmem, vmem],
        out_specs=(pl.BlockSpec((1, 8, 256), lambda i: (i, 0, 0)),
                   pl.BlockSpec((1, 256, WIDTH), lambda i: (i, 0, 0)), vmem, smem),
        scratch_shapes=[pltpu.VMEM((320, 128), jnp.float32),
                        pltpu.VMEM((2, 8, 2, 4, ACC_ROWS, 128), jnp.float32)],
        compiler_params=pltpu.CompilerParams(vmem_limit_bytes=28 << 20),
        name="score_slots",
    )(cands, priors, unit, images, refs)


def norm_kernel(stats, total, boxes, ssem, rsem):
    me = lax.axis_index("cls")
    barrier = pltpu.get_barrier_semaphore()
    for k in range(1, GROUPS):
        pl.semaphore_signal(barrier, inc=1, device_id={"cls": (me + k) % GROUPS}, device_id_type=MESH)
    pl.semaphore_wait(barrier, GROUPS - 1)
    copies = []
    for k in range(1, GROUPS):
        copy = pltpu.make_async_remote_copy(src_ref=stats, dst_ref=boxes.at[k - 1], send_sem=ssem.at[k - 1],
                                            recv_sem=rsem.at[k - 1], device_id={"cls": (me + k) % GROUPS},
                                            device_id_type=MESH)
        copy.start()
        copies.append(copy)
    for copy in copies:
        copy.wait_recv()
    best = stats[0:1, :]
    for k in range(GROUPS - 1):
        best = jnp.maximum(best, boxes[k, 0:1, :])
    whole = stats[1:2, :] * jnp.exp(stats[0:1, :] - best)
    for k in range(GROUPS - 1):
        whole = whole + boxes[k, 1:2, :] * jnp.exp(boxes[k, 0:1, :] - best)
    total[...] = jnp.concatenate([best, whole, jnp.zeros((6, 128), jnp.float32)], axis=0)
    for copy in copies:
        copy.wait_send()


def normalise(stats):
    vmem = pl.BlockSpec(memory_space=pltpu.VMEM)
    return pl.pallas_call(
        norm_kernel,
        out_shape=jax.ShapeDtypeStruct((8, 128), jnp.float32),
        in_specs=[vmem],
        out_specs=vmem,
        scratch_shapes=[pltpu.VMEM((GROUPS - 1, 8, 128), jnp.float32),
                        pltpu.SemaphoreType.DMA((7,)), pltpu.SemaphoreType.DMA((7,))],
        compiler_params=pltpu.CompilerParams(collective_id=2, has_side_effects=True, vmem_limit_bytes=4 << 20),
        name="normalise",
    )(stats)


def sum_kernel(table, total, scores, moved, out, acc, comp, masses):
    slot = pl.program_id(0)

    @pl.when(slot == 0)
    def _():
        acc[...] = jnp.zeros(acc.shape, jnp.float32)
        masses[...] = jnp.zeros(masses.shape, jnp.float32)

    @pl.when(table[slot * 8 + 5] > 0)
    def _():
        pid = table[slot * 8 + 6]
        place = lax.broadcasted_iota(jnp.int32, (1, 128), 1) == pid
        best = jnp.sum(jnp.where(place, total[0:1, :], 0.0), axis=1, keepdims=True)
        whole = jnp.sum(jnp.where(place, total[1:2, :], 0.0), axis=1, keepdims=True)
        row, _, turn = lane_places(ACC_ROWS)
        later = turn >= row
        halves = []
        mass = jnp.zeros((8, 1), jnp.float32)
        for half in range(2):
            weight = jnp.exp(scores[0, :, 128 * half:128 * half + 128] - best) / whole
            weight = weight.astype(jnp.bfloat16).astype(jnp.float32)
            mass = mass + jnp.sum(weight, axis=1, keepdims=True)
            back = pltpu.roll(weight, 92, 1)
            rows = []
            for k in range(4):
                one = jnp.broadcast_to(weight[k:k + 1, :], (ACC_ROWS, 128))
                two = jnp.broadcast_to(back[k:k + 1, :], (ACC_ROWS, 128))
                rows.append(jnp.where(later, pltpu.roll(one, 0, 1, stride=1, stride_axis=0),
                                      pltpu.roll(two, 0, 1, stride=1, stride_axis=0)))
            halves.append(jnp.concatenate(rows, axis=0))
        spread = jnp.concatenate(halves, axis=1).astype(jnp.bfloat16)
        for k in range(4):
            c = table[slot * 8 + k]
            masses[pl.ds(c, 1), :] = masses[pl.ds(c, 1), :] + jnp.broadcast_to(mass[k:k + 1, :], (1, 128))
        contrib = jnp.dot(spread, moved[0], preferred_element_type=jnp.float32)
        for k in range(4):
            c = table[slot * 8 + k]
            acc[c] = acc[c] + contrib[ACC_ROWS * k:ACC_ROWS * (k + 1)]

    @pl.when(slot == SLOTS - 1)
    def _():
        row = lax.broadcasted_iota(jnp.int32, (32, 128), 0)
        lane = lax.broadcasted_iota(jnp.int32, (32, 128), 1)
        line = jnp.sum(jnp.where(row == lane, masses[...], 0.0), axis=0, keepdims=True)
        high = line.astype(jnp.bfloat16).astype(jnp.float32)
        lead = jnp.concatenate([high, line - high, jnp.zeros((14, 128), jnp.float32)], axis=0)
        for y in range(4):
            comp[y * 240:y * 240 + 16, :] = jnp.concatenate([lead] * 8, axis=1)
        for c in range(CLS_LOC):
            start = c * ROTS
            while start < (c + 1) * ROTS:
                y = start // DROWS
                stop = min((c + 1) * ROTS, (y + 1) * DROWS)
                to = y * 240 + LEAD + start - y * DROWS
                comp[to:to + stop - start, :] = acc[c, start - c * ROTS:stop - c * ROTS, :]
                start = stop
        for ch in range(NCH):
            for y in range(4):
                for z in range(8):
                    out[ch, y, z] = comp[y * 240 + ch * RC:y * 240 + (ch + 1) * RC,
                                         128 * z:128 * z + 128].astype(jnp.bfloat16)


def sum_slots(table, total, scores, moved):
    vmem, smem = pl.BlockSpec(memory_space=pltpu.VMEM), pl.BlockSpec(memory_space=pltpu.SMEM)
    return pl.pallas_call(
        sum_kernel,
        grid=(SLOTS,),
        out_shape=jax.ShapeDtypeStruct((NCH, 4, 8, RC, 128), jnp.bfloat16),
        in_specs=[smem, vmem, pl.BlockSpec((1, 8, 256), lambda i: (i, 0, 0)),
                  pl.BlockSpec((1, 256, WIDTH), lambda i: (i, 0, 0))],
        out_specs=vmem,
        scratch_shapes=[pltpu.VMEM((CLS_LOC, ACC_ROWS, WIDTH), jnp.float32),
                        pltpu.VMEM((960, WIDTH), jnp.float32),
                        pltpu.VMEM((32, 128), jnp.float32)],
        compiler_params=pltpu.CompilerParams(vmem_limit_bytes=28 << 20),
        name="sum_slots",
    )(table, total, scores, moved)


def reduce_kernel(p_ref, g_ref, x1, x2, d3, d4, e5, e6, c1, c2, s_buf, z_buf, ysend, yrecv, zsend, zrecv):
    dom = lax.axis_index("dom")
    y = dom % 4
    z = dom // 4
    yp, ym, yo = (y + 1) % 4, (y + 3) % 4, (y + 2) % 4
    up, down = {"dom": z * 4 + yp}, {"dom": z * 4 + ym}
    zdev = [{"dom": ((z + k) % 8) * 4 + y} for k in range(8)]
    barrier = pltpu.get_barrier_semaphore()
    for target in [up, down] + zdev[1:]:
        pl.semaphore_signal(barrier, inc=1, device_id=target, device_id_type=MESH)
    pl.semaphore_wait(barrier, 9)
    A, B = pl.ds(0, 4), pl.ds(4, 4)

    def send(src, dst, ssem, rsem, target):
        copy = pltpu.make_async_remote_copy(src_ref=src, dst_ref=dst, send_sem=ssem, recv_sem=rsem,
                                            device_id=target, device_id_type=MESH)
        copy.start()
        return copy

    m1, m2, m3, m4, m5, m6 = {}, {}, {}, {}, {}, {}
    zm, zg, m7, m8, m9, m10 = {}, {}, {}, {}, {}, {}
    masses = []

    def far(ch):
        m1[ch] = send(p_ref.at[ch, yo, A], x1.at[ch], ysend.at[ch, 0], yrecv.at[ch, 0], up)
        m2[ch] = send(p_ref.at[ch, yo, B], x2.at[ch], ysend.at[ch, 1], yrecv.at[ch, 1], down)

    def near(ch):
        m3[ch] = send(p_ref.at[ch, yp, B], d3.at[ch], ysend.at[ch, 2], yrecv.at[ch, 2], up)
        m4[ch] = send(p_ref.at[ch, ym, A], d4.at[ch], ysend.at[ch, 3], yrecv.at[ch, 3], down)

    def relay(ch):
        m1[ch].wait_recv()
        c1[ch] = (x1[ch].astype(jnp.float32) + p_ref[ch, yp, A].astype(jnp.float32)).astype(jnp.bfloat16)
        m5[ch] = send(c1.at[ch], e5.at[ch], ysend.at[ch, 4], yrecv.at[ch, 4], up)
        m2[ch].wait_recv()
        c2[ch] = (x2[ch].astype(jnp.float32) + p_ref[ch, ym, B].astype(jnp.float32)).astype(jnp.bfloat16)
        m6[ch] = send(c2.at[ch], e6.at[ch], ysend.at[ch, 5], yrecv.at[ch, 5], down)

    def column(ch):
        m4[ch].wait_recv()
        m5[ch].wait_recv()
        s_buf[ch, A] = (p_ref[ch, y, A].astype(jnp.float32) + e5[ch].astype(jnp.float32)
                        + d4[ch].astype(jnp.float32)).astype(jnp.bfloat16)
        m3[ch].wait_recv()
        m6[ch].wait_recv()
        s_buf[ch, B] = (p_ref[ch, y, B].astype(jnp.float32) + e6[ch].astype(jnp.float32)
                        + d3[ch].astype(jnp.float32)).astype(jnp.bfloat16)
        for k in (4, 3, 5, 2, 6, 1, 7):
            zm[ch, k] = send(s_buf.at[ch, (z + k) % 8], z_buf.at[ch, k - 1],
                             zsend.at[ch, k - 1], zrecv.at[ch, k - 1], zdev[k])

    def finish(ch):
        num = s_buf[ch, z].astype(jnp.float32)
        for k in range(1, 8):
            zm[ch, k].wait_recv()
            num = num + z_buf[ch, k - 1].astype(jnp.float32)
        if ch == 0:
            masses.append(num[0:1, :] + num[1:2, :] + 1.0)
        mass = masses[0]
        place = DROWS * y + (ch * RC - LEAD) + lax.broadcasted_iota(jnp.int32, (RC, 128), 0)
        den = jnp.ones((RC, 128), jnp.float32)
        for c in range(CLS_LOC):
            here = (place >= c * ROTS) & (place < (c + 1) * ROTS)
            den = jnp.where(here, jnp.broadcast_to(mass[:, c:c + 1], (RC, 128)), den)
        g_ref[ch, y, z] = (num / den).astype(jnp.bfloat16)
        for k in (4, 3, 5, 2, 6, 1, 7):
            zg[ch, k] = send(g_ref.at[ch, y, z], g_ref.at[ch, y, z],
                             zsend.at[ch, 6 + k], zrecv.at[ch, 6 + k], zdev[k])

    def share(ch):
        for k in range(1, 8):
            zg[ch, k].wait_recv()
        m7[ch] = send(g_ref.at[ch, y], g_ref.at[ch, y], ysend.at[ch, 6], yrecv.at[ch, 6], up)
        m8[ch] = send(g_ref.at[ch, y], g_ref.at[ch, y], ysend.at[ch, 7], yrecv.at[ch, 7], down)

    def pass_on(ch):
        m7[ch].wait_recv()
        m9[ch] = send(g_ref.at[ch, ym, A], g_ref.at[ch, ym, A], ysend.at[ch, 8], yrecv.at[ch, 8], up)
        m8[ch].wait_recv()
        m10[ch] = send(g_ref.at[ch, yp, B], g_ref.at[ch, yp, B], ysend.at[ch, 9], yrecv.at[ch, 9], down)

    far(0)
    near(0)
    for step in range(NCH + 4):
        if step + 1 < NCH:
            far(step + 1)
        for lag, stage in enumerate((relay, column, finish, share, pass_on)):
            if stage is column and step + 1 < NCH:
                near(step + 1)
            if 0 <= step - lag < NCH:
                stage(step - lag)
    for ch in range(NCH):
        m9[ch].wait_recv()
        m10[ch].wait_recv()
    for group in (m1, m2, m3, m4, m5, m6, zm, zg, m7, m8, m9, m10):
        for copy in group.values():
            copy.wait_send()


def reduce_average(payload):
    half = pltpu.VMEM((NCH, 4, RC, 128), jnp.bfloat16)
    return pl.pallas_call(
        reduce_kernel,
        out_shape=jax.ShapeDtypeStruct((NCH, 4, 8, RC, 128), jnp.bfloat16),
        in_specs=[pl.BlockSpec(memory_space=pltpu.VMEM)],
        out_specs=pl.BlockSpec(memory_space=pltpu.VMEM),
        scratch_shapes=[half] * 8 + [
            pltpu.VMEM((NCH, 8, RC, 128), jnp.bfloat16),
            pltpu.VMEM((NCH, 7, RC, 128), jnp.bfloat16),
            pltpu.SemaphoreType.DMA((NCH, 10)),
            pltpu.SemaphoreType.DMA((NCH, 10)),
            pltpu.SemaphoreType.DMA((NCH, 14)),
            pltpu.SemaphoreType.DMA((NCH, 14)),
        ],
        compiler_params=pltpu.CompilerParams(collective_id=5, has_side_effects=True, vmem_limit_bytes=40 << 20),
        name="reduce_average",
    )(payload)


def unpack_average(gathered):
    rows = gathered.transpose(1, 0, 3, 2, 4).reshape(4, NCH * RC, 8, 128)[:, LEAD:]
    return rows.reshape(CLS_LOC, 36864)


def shards(particles, references, candidates, offsets):
    images, cands, priors, refs = gather_particles(particles.reshape(PART, 288, 128), candidates, offsets, references)
    scores, moved, stats, table = score_slots(cands, priors, jnp.asarray(unit_tables()), images, refs)
    payload = sum_slots(table, normalise(stats), scores, moved)
    return unpack_average(reduce_average(payload))


def solution(mesh):
    in_specs = (
        P(("cls", "dom"), None),
        P("cls", None),
        P(("cls", "dom"), None),
        P(("cls", "dom"), None),
    )
    return jax.shard_map(shards, mesh=mesh, in_specs=in_specs, out_specs=P("cls", None), check_vma=False)
```

```python
import math
import numpy as np
import jax, jax.numpy as jnp
from jax import lax
from jax.experimental import pallas as pl
from jax.experimental.pallas import tpu as pltpu
from jax.sharding import PartitionSpec as P

MESH = pl.DeviceIdType.MESH
CYCLES, ANGLES, ROTS, SHIFTS, BOX = 128, 144, 36, 5, 256
CLS_LOC, NCH, RC, LEAD, DROWS = 25, 5, 48, 15, 225
GROUPS, SLOTS, PART = 8, 16, 4
NEGATIVE = -1e30
WIDTH, LHS_ROWS, ACC_ROWS = 1024, 48, 40


def unit_tables():
    angle = 2.0 * math.pi * np.arange(ANGLES) / ANGLES
    radius = np.arange(1, CYCLES + 1)
    out = np.zeros((2, 2, 4, ACC_ROWS, CYCLES), np.float64)
    for axis, along in enumerate((np.cos(angle), np.sin(angle))):
        phase = (2.0 * math.pi / BOX) * along[:, None] * radius
        for part, value in enumerate((np.cos(phase), np.sin(phase))):
            out[axis, part, :, :ROTS] = value.reshape(ROTS, 4, CYCLES).transpose(1, 0, 2)
    return out.astype(np.float32)


def gather_kernel(p_ref, cand_ref, offs_ref, refs_ref, unit, out_ref, cout_ref, oout_ref, rows_ref, powers, flat, tall, lsem, ssem, rsem):
    me = lax.axis_index("cls")
    core = me % 2
    right, left, across = (me + 2) % GROUPS, (me + 6) % GROUPS, (me + 4) % GROUPS
    pair = me + 1 - 2 * core
    shift = pair - me
    barrier = pltpu.get_barrier_semaphore()
    for k in range(1, GROUPS):
        pl.semaphore_signal(barrier, inc=1, device_id={"cls": (me + k) % GROUPS}, device_id_type=MESH)
    pl.semaphore_wait(barrier, GROUPS - 1)
    h0, h1 = pl.ds(0, 2), pl.ds(2, 2)
    sends = []

    def send(src, dst, i, target):
        copy = pltpu.make_async_remote_copy(src_ref=src, dst_ref=dst, send_sem=ssem.at[i], recv_sem=rsem.at[i],
                                            device_id={"cls": target}, device_id_type=MESH)
        copy.start()
        sends.append(copy)
        return copy

    metas = [send(cand_ref, cout_ref.at[me], 12 + k, (me + k) % GROUPS) for k in range(1, GROUPS)]
    metas += [send(offs_ref, oout_ref.at[me], 19 + k, (me + k) % GROUPS) for k in range(1, GROUPS)]
    r0 = send(p_ref.at[h0], out_ref.at[me, h0], 0, right)
    l1 = send(p_ref.at[h1], out_ref.at[me, h1], 1, left)
    r1 = send(p_ref.at[h1], out_ref.at[me, h1], 2, right)
    l0 = send(p_ref.at[h0], out_ref.at[me, h0], 3, left)
    own = send(p_ref, out_ref.at[me], 4, pair)
    locals_ = [pltpu.make_async_copy(p_ref, out_ref.at[me], lsem.at[0]),
               pltpu.make_async_copy(cand_ref, cout_ref.at[me], lsem.at[1]),
               pltpu.make_async_copy(offs_ref, oout_ref.at[me], lsem.at[2])]
    fetch = pltpu.make_async_copy(refs_ref, flat, lsem.at[3])
    fetch.start()
    for copy in locals_:
        copy.start()

    def clear(c, carry):
        for g in range(8):
            tall[g, pl.ds(pl.multiple_of(c * LHS_ROWS + 32, 16), 16), :] = jnp.zeros((16, 128), jnp.float32)
        return carry

    def spread(l, carry):
        value = flat[:, pl.ds(pl.multiple_of(l * WIDTH, WIDTH), WIDTH)].astype(jnp.float32)
        for g in range(8):
            tall[g, pl.ds(ROTS - 1 - l, CLS_LOC, stride=LHS_ROWS), :] = value[:, 128 * g:128 * g + 128]
        return carry

    def pack(c, carry):
        rows = pl.ds(pl.multiple_of(c * LHS_ROWS, LHS_ROWS), LHS_ROWS)
        for g in range(8):
            rows_ref[c, :, 128 * g:128 * g + 128] = tall[g, rows, :].astype(jnp.bfloat16)
        return carry

    lax.fori_loop(0, CLS_LOC, clear, 0)
    fetch.wait()
    lax.fori_loop(0, ROTS, spread, 0)
    r0.wait_recv()
    fr = send(out_ref.at[left, h0], out_ref.at[left, h0], 5, right)
    s0 = send(out_ref.at[left, h0], out_ref.at[left, h0], 7, pair)
    l1.wait_recv()
    fl = send(out_ref.at[right, h1], out_ref.at[right, h1], 6, left)
    s1 = send(out_ref.at[right, h1], out_ref.at[right, h1], 8, pair)
    lax.fori_loop(0, CLS_LOC, pack, 0)
    for axis in range(2):
        powers[axis, 0, 0] = jnp.ones((4, ACC_ROWS, 128), jnp.float32)
        powers[axis, 0, 1] = jnp.zeros((4, ACC_ROWS, 128), jnp.float32)
        powers[axis, 1] = unit[axis]
        for t in range(2, 8):
            pc, ps = powers[axis, t - 1, 0], powers[axis, t - 1, 1]
            qc, qs = unit[axis, 0], unit[axis, 1]
            powers[axis, t, 0] = pc * qc - ps * qs
            powers[axis, t, 1] = ps * qc + pc * qs
    r1.wait_recv()
    s2 = send(out_ref.at[left, h1], out_ref.at[left, h1], 9, pair)
    l0.wait_recv()
    s3 = send(out_ref.at[right, h0], out_ref.at[right, h0], 10, pair)
    fr.wait_recv()
    s4 = send(out_ref.at[across, h0], out_ref.at[across, h0], 11, pair)
    fl.wait_recv()
    s5 = send(out_ref.at[across, h1], out_ref.at[across, h1], 12, pair)
    for copy in [own, s0, s1, s2, s3, s4, s5] + metas:
        copy.wait_recv()
    for copy in locals_:
        copy.wait()
    for copy in sends:
        copy.wait_send()


def gather_particles(images, candidates, offsets, refs, unit):
    vmem = pl.BlockSpec(memory_space=pltpu.VMEM)
    return pl.pallas_call(
        gather_kernel,
        out_shape=(jax.ShapeDtypeStruct((GROUPS, PART, 288, 128), jnp.bfloat16),
                   jax.ShapeDtypeStruct((GROUPS, PART, 8), jnp.int32),
                   jax.ShapeDtypeStruct((GROUPS, 2, PART), jnp.int32),
                   jax.ShapeDtypeStruct((CLS_LOC, LHS_ROWS, WIDTH), jnp.bfloat16),
                   jax.ShapeDtypeStruct((2, 8, 2, 4, ACC_ROWS, 128), jnp.float32)),
        in_specs=[vmem] + [pl.BlockSpec(memory_space=pltpu.HBM)] * 3 + [vmem],
        out_specs=(vmem,) * 5,
        scratch_shapes=[pltpu.VMEM((CLS_LOC, ROTS * WIDTH), jnp.bfloat16), pltpu.VMEM((8, CLS_LOC * LHS_ROWS, 128), jnp.float32), pltpu.SemaphoreType.DMA((4,)),
                        pltpu.SemaphoreType.DMA((27,)), pltpu.SemaphoreType.DMA((27,))],
        compiler_params=pltpu.CompilerParams(collective_id=1, has_side_effects=True, vmem_limit_bytes=24 << 20),
        name="gather_particles",
    )(images, candidates, offsets, refs, unit)


def group_turn(lane):
    return lane - jnp.where(lane >= 80, 80, jnp.where(lane >= 40, 40, 0))


def lane_places(rows):
    row = lax.broadcasted_iota(jnp.int32, (rows, 128), 0)
    lane = lax.broadcasted_iota(jnp.int32, (rows, 128), 1)
    return row, lane, group_turn(lane)


def score_kernel(cands, priors, powers, images, refs, scores, moved, stats, table, wide):
    owner = lax.axis_index("cls")
    base = jnp.int32(0)
    for pid in range(GROUPS * PART):
        spot = base
        for t in range(8):
            c = cands[pid // PART, pid % PART, t] - owner * CLS_LOC
            table[spot] = c
            spot = spot + jnp.where(c.astype(jnp.uint32) < CLS_LOC, 1, 0)
        table[base + 6] = pid
        base = base + jnp.where(spot > base, 8, 0)
    place = base // 8
    table[SLOTS * 8 + 7] = place
    wide[288:320, :] = jnp.zeros((32, 128), jnp.float32)
    first = lax.broadcasted_iota(jnp.int32, (8, 128), 0) == 0
    stats[...] = jnp.where(first, NEGATIVE, 0.0)

    def one_slot(slot, carry):
        pid = table[slot * 8 + 6]
        v, i = pid // PART, pid % PART
        tx, ty = priors[v, 0, i], priors[v, 1, i]
        ax, ay = jnp.abs(tx), jnp.abs(ty)
        gx = jnp.where(tx < 0, -1.0, 1.0).astype(jnp.float32)
        gy = jnp.where(ty < 0, -1.0, 1.0).astype(jnp.float32)
        wide[0:288, :] = images[v, i].astype(jnp.float32)
        gap8, gap48 = jnp.zeros((8, 128), jnp.float32), jnp.zeros((48, 128), jnp.float32)
        for a in range(4):
            re = wide[pl.ds(2 * a, ACC_ROWS, stride=8), :]
            im = wide[pl.ds(2 * a + 1, ACC_ROWS, stride=8), :]
            cx, sx = powers[0, ax, 0, a], powers[0, ax, 1, a] * gx
            cy, sy = powers[1, ay, 0, a], powers[1, ay, 1, a] * gy
            bc, bs = cx * cy - sx * sy, sx * cy + cx * sy
            zr, zi = re * bc + im * bs, im * bc - re * bs
            real, imag = [zr], [zi]
            for axis in range(2):
                uc, us = powers[axis, 1, 0, a], powers[axis, 1, 1, a]
                rc, rs, ic, js = zr * uc, zr * us, zi * uc, zi * us
                real += [rc + js, rc - js]
                imag += [ic - rs, ic + rs]
            for m, part in enumerate((real, imag)):
                lanes = pl.ds(256 * a + 128 * m, 128)
                moved[slot, 0:128, lanes] = jnp.concatenate(part[0:3] + [gap8], axis=0).astype(jnp.bfloat16)
                moved[slot, 128:256, lanes] = jnp.concatenate(part[3:5] + [gap48], axis=0).astype(jnp.bfloat16)
        lhs = jnp.concatenate([refs[table[slot * 8 + k]] for k in range(4)], axis=0)
        pairs = lax.dot_general(lhs, moved[slot], (((1,), (1,)), ((), ())), preferred_element_type=jnp.float32)
        row = lax.broadcasted_iota(jnp.int32, (ACC_ROWS, 128), 0)
        lane = lax.broadcasted_iota(jnp.int32, (ACC_ROWS, 128), 1)
        turn = group_turn(jnp.where(lane >= ROTS - 1, lane - (ROTS - 1), lane + 128 - (ROTS - 1)))
        turn2 = group_turn(jnp.where(lane == 127, 0, lane + 1))
        back = (ROTS - 1) - row
        direct = (turn + back < ROTS) & (back >= 0)
        wrapped = (turn2 < ROTS) & (turn2 + back >= ROTS)
        _, lane1, turn1 = lane_places(8)
        lines = []
        for half in range(2):
            rows = []
            for k in range(4):
                block = pairs[LHS_ROWS * k:LHS_ROWS * k + ACC_ROWS, 128 * half:128 * half + 128]
                skew = pltpu.roll(block, 0, 1, stride=1, stride_axis=0)
                near = jnp.sum(jnp.where(direct, skew, 0.0), axis=0, keepdims=True)
                far = jnp.sum(jnp.where(wrapped, skew, 0.0), axis=0, keepdims=True)
                rows.append((near, far))
            near = jnp.concatenate([r[0] for r in rows] + [jnp.zeros((4, 128), jnp.float32)], axis=0)
            far = jnp.concatenate([r[1] for r in rows] + [jnp.zeros((4, 128), jnp.float32)], axis=0)
            whole = 2.0 * (pltpu.roll(near, 128 - (ROTS - 1), 1) + pltpu.roll(far, 1, 1))
            row8 = lax.broadcasted_iota(jnp.int32, (8, 128), 0)
            good = (turn1 < ROTS) & (lane1 < (120 if half == 0 else 80)) & (row8 < 4)
            line = jnp.where(good, whole, NEGATIVE)
            scores[slot, :, 128 * half:128 * half + 128] = line
            lines.append(line)
        best = jnp.max(jnp.max(jnp.maximum(lines[0], lines[1]), axis=1, keepdims=True), axis=0, keepdims=True)
        power = jnp.exp(lines[0] - best) + jnp.exp(lines[1] - best)
        mass = jnp.sum(jnp.sum(power, axis=1, keepdims=True), axis=0, keepdims=True)
        here = lax.broadcasted_iota(jnp.int32, (1, 128), 1) == pid
        stats[0:1, :] = jnp.where(here, best, stats[0:1, :])
        stats[1:2, :] = jnp.where(here, mass, stats[1:2, :])
        return carry

    lax.fori_loop(0, place, one_slot, 0)


def score_slots(cands, priors, powers, images, refs):
    vmem, smem = pl.BlockSpec(memory_space=pltpu.VMEM), pl.BlockSpec(memory_space=pltpu.SMEM)
    return pl.pallas_call(
        score_kernel,
        out_shape=(jax.ShapeDtypeStruct((SLOTS, 8, 256), jnp.float32),
                   jax.ShapeDtypeStruct((SLOTS, 256, WIDTH), jnp.bfloat16),
                   jax.ShapeDtypeStruct((8, 128), jnp.float32),
                   jax.ShapeDtypeStruct(((SLOTS + 1) * 8,), jnp.int32)),
        in_specs=[smem, smem, vmem, vmem, vmem],
        out_specs=(vmem, vmem, vmem, smem),
        scratch_shapes=[pltpu.VMEM((320, 128), jnp.float32)],
        compiler_params=pltpu.CompilerParams(vmem_limit_bytes=32 << 20),
        name="score_slots",
    )(cands, priors, powers, images, refs)


def norm_kernel(stats, total, boxes, ssem, rsem):
    me = lax.axis_index("cls")
    barrier = pltpu.get_barrier_semaphore()
    for k in range(1, GROUPS):
        pl.semaphore_signal(barrier, inc=1, device_id={"cls": (me + k) % GROUPS}, device_id_type=MESH)
    pl.semaphore_wait(barrier, GROUPS - 1)
    copies = []
    for k in range(1, GROUPS):
        copy = pltpu.make_async_remote_copy(src_ref=stats, dst_ref=boxes.at[k - 1], send_sem=ssem.at[k - 1],
                                            recv_sem=rsem.at[k - 1], device_id={"cls": (me + k) % GROUPS},
                                            device_id_type=MESH)
        copy.start()
        copies.append(copy)
    for copy in copies:
        copy.wait_recv()
    best = stats[0:1, :]
    for k in range(GROUPS - 1):
        best = jnp.maximum(best, boxes[k, 0:1, :])
    whole = stats[1:2, :] * jnp.exp(stats[0:1, :] - best)
    for k in range(GROUPS - 1):
        whole = whole + boxes[k, 1:2, :] * jnp.exp(boxes[k, 0:1, :] - best)
    total[...] = jnp.concatenate([best, whole, jnp.zeros((6, 128), jnp.float32)], axis=0)
    for copy in copies:
        copy.wait_send()


def normalise(stats):
    vmem = pl.BlockSpec(memory_space=pltpu.VMEM)
    return pl.pallas_call(
        norm_kernel,
        out_shape=jax.ShapeDtypeStruct((8, 128), jnp.float32),
        in_specs=[vmem],
        out_specs=vmem,
        scratch_shapes=[pltpu.VMEM((GROUPS - 1, 8, 128), jnp.float32),
                        pltpu.SemaphoreType.DMA((7,)), pltpu.SemaphoreType.DMA((7,))],
        compiler_params=pltpu.CompilerParams(collective_id=2, has_side_effects=True, vmem_limit_bytes=4 << 20),
        name="normalise",
    )(stats)


def sum_kernel(table, total, scores, moved, out, acc, comp, masses, spread):
    filled = table[SLOTS * 8 + 7]
    acc[...] = jnp.zeros(acc.shape, jnp.float32)
    masses[...] = jnp.zeros(masses.shape, jnp.float32)

    def prepare(slot, count):
        pid = table[slot * 8 + 6]
        place = lax.broadcasted_iota(jnp.int32, (1, 128), 1) == pid
        best = jnp.sum(jnp.where(place, total[0:1, :], 0.0), axis=1, keepdims=True)
        whole = jnp.sum(jnp.where(place, total[1:2, :], 0.0), axis=1, keepdims=True)
        row, _, turn = lane_places(ACC_ROWS)
        later = turn >= row
        halves = []
        mass = jnp.zeros((8, 1), jnp.float32)
        for half in range(2):
            weight = jnp.exp(scores[slot, :, 128 * half:128 * half + 128] - best) / whole
            weight = weight.astype(jnp.bfloat16).astype(jnp.float32)
            mass = mass + jnp.sum(weight, axis=1, keepdims=True)
            back = pltpu.roll(weight, 92, 1)
            rows = []
            for k in range(4):
                one = jnp.broadcast_to(weight[k:k + 1, :], (ACC_ROWS, 128))
                two = jnp.broadcast_to(back[k:k + 1, :], (ACC_ROWS, 128))
                rows.append(jnp.where(later, pltpu.roll(one, 0, 1, stride=1, stride_axis=0),
                                      pltpu.roll(two, 0, 1, stride=1, stride_axis=0)))
            halves.append(jnp.concatenate(rows, axis=0))
        spread[slot % 2] = jnp.concatenate(halves, axis=1).astype(jnp.bfloat16)
        for k in range(4):
            c = table[slot * 8 + k]
            masses[pl.ds(c, 1), :] = masses[pl.ds(c, 1), :] + count * jnp.broadcast_to(mass[k:k + 1, :], (1, 128))

    def one_slot(slot, carry):
        contrib = jnp.dot(spread[slot % 2], moved[slot], preferred_element_type=jnp.float32)
        prepare(jnp.minimum(slot + 1, filled - 1), jnp.where(slot + 1 < filled, 1.0, 0.0))
        for k in range(4):
            c = table[slot * 8 + k]
            acc[c] = acc[c] + contrib[ACC_ROWS * k:ACC_ROWS * (k + 1)]
        return carry

    @pl.when(filled > 0)
    def _():
        prepare(0, 1.0)
        lax.fori_loop(0, filled, one_slot, 0)

    row = lax.broadcasted_iota(jnp.int32, (32, 128), 0)
    lane = lax.broadcasted_iota(jnp.int32, (32, 128), 1)
    line = jnp.sum(jnp.where(row == lane, masses[...], 0.0), axis=0, keepdims=True)
    high = line.astype(jnp.bfloat16).astype(jnp.float32)
    lead = jnp.concatenate([high, line - high, jnp.zeros((14, 128), jnp.float32)], axis=0)
    for y in range(4):
        comp[y * 240:y * 240 + 16, :] = jnp.concatenate([lead] * 8, axis=1)
    for c in range(CLS_LOC):
        start = c * ROTS
        while start < (c + 1) * ROTS:
            y = start // DROWS
            stop = min((c + 1) * ROTS, (y + 1) * DROWS)
            to = y * 240 + LEAD + start - y * DROWS
            comp[to:to + stop - start, :] = acc[c, start - c * ROTS:stop - c * ROTS, :]
            start = stop
    for ch in range(NCH):
        for y in range(4):
            for z in range(8):
                out[ch, y, z] = comp[y * 240 + ch * RC:y * 240 + (ch + 1) * RC,
                                     128 * z:128 * z + 128].astype(jnp.bfloat16)


def sum_slots(table, total, scores, moved):
    vmem, smem = pl.BlockSpec(memory_space=pltpu.VMEM), pl.BlockSpec(memory_space=pltpu.SMEM)
    return pl.pallas_call(
        sum_kernel,
        out_shape=jax.ShapeDtypeStruct((NCH, 4, 8, RC, 128), jnp.bfloat16),
        in_specs=[smem, vmem, vmem, vmem],
        out_specs=vmem,
        scratch_shapes=[pltpu.VMEM((CLS_LOC, ACC_ROWS, WIDTH), jnp.float32),
                        pltpu.VMEM((960, WIDTH), jnp.float32),
                        pltpu.VMEM((32, 128), jnp.float32),
                        pltpu.VMEM((2, 4 * ACC_ROWS, 256), jnp.bfloat16)],
        compiler_params=pltpu.CompilerParams(vmem_limit_bytes=32 << 20),
        name="sum_slots",
    )(table, total, scores, moved)


def reduce_kernel(p_ref, g_ref, x1, x2, d3, d4, e5, e6, c1, c2, s_buf, z_buf, ysend, yrecv, zsend, zrecv):
    dom = lax.axis_index("dom")
    y = dom % 4
    z = dom // 4
    yp, ym, yo = (y + 1) % 4, (y + 3) % 4, (y + 2) % 4
    up, down = {"dom": z * 4 + yp}, {"dom": z * 4 + ym}
    zdev = [{"dom": ((z + k) % 8) * 4 + y} for k in range(8)]
    barrier = pltpu.get_barrier_semaphore()
    for target in [up, down] + zdev[1:]:
        pl.semaphore_signal(barrier, inc=1, device_id=target, device_id_type=MESH)
    pl.semaphore_wait(barrier, 9)
    A, B = pl.ds(0, 4), pl.ds(4, 4)

    def send(src, dst, ssem, rsem, target):
        copy = pltpu.make_async_remote_copy(src_ref=src, dst_ref=dst, send_sem=ssem, recv_sem=rsem,
                                            device_id=target, device_id_type=MESH)
        copy.start()
        return copy

    m1, m2, m3, m4, m5, m6 = {}, {}, {}, {}, {}, {}
    zm, zg, m7, m8, m9, m10 = {}, {}, {}, {}, {}, {}
    masses = []

    def far(ch):
        m1[ch] = send(p_ref.at[ch, yo, A], x1.at[ch], ysend.at[ch, 0], yrecv.at[ch, 0], up)
        m2[ch] = send(p_ref.at[ch, yo, B], x2.at[ch], ysend.at[ch, 1], yrecv.at[ch, 1], down)

    def near(ch):
        m3[ch] = send(p_ref.at[ch, yp, B], d3.at[ch], ysend.at[ch, 2], yrecv.at[ch, 2], up)
        m4[ch] = send(p_ref.at[ch, ym, A], d4.at[ch], ysend.at[ch, 3], yrecv.at[ch, 3], down)

    def relay(ch):
        m1[ch].wait_recv()
        c1[ch] = (x1[ch].astype(jnp.float32) + p_ref[ch, yp, A].astype(jnp.float32)).astype(jnp.bfloat16)
        m5[ch] = send(c1.at[ch], e5.at[ch], ysend.at[ch, 4], yrecv.at[ch, 4], up)
        m2[ch].wait_recv()
        c2[ch] = (x2[ch].astype(jnp.float32) + p_ref[ch, ym, B].astype(jnp.float32)).astype(jnp.bfloat16)
        m6[ch] = send(c2.at[ch], e6.at[ch], ysend.at[ch, 5], yrecv.at[ch, 5], down)

    def column(ch):
        m4[ch].wait_recv()
        m5[ch].wait_recv()
        s_buf[ch, A] = (p_ref[ch, y, A].astype(jnp.float32) + e5[ch].astype(jnp.float32)
                        + d4[ch].astype(jnp.float32)).astype(jnp.bfloat16)
        m3[ch].wait_recv()
        m6[ch].wait_recv()
        s_buf[ch, B] = (p_ref[ch, y, B].astype(jnp.float32) + e6[ch].astype(jnp.float32)
                        + d3[ch].astype(jnp.float32)).astype(jnp.bfloat16)
        for k in (4, 3, 5, 2, 6, 1, 7):
            zm[ch, k] = send(s_buf.at[ch, (z + k) % 8], z_buf.at[ch, k - 1],
                             zsend.at[ch, k - 1], zrecv.at[ch, k - 1], zdev[k])

    def finish(ch):
        num = s_buf[ch, z].astype(jnp.float32)
        for k in range(1, 8):
            zm[ch, k].wait_recv()
            num = num + z_buf[ch, k - 1].astype(jnp.float32)
        if ch == 0:
            masses.append(num[0:1, :] + num[1:2, :] + 1.0)
        mass = masses[0]
        place = DROWS * y + (ch * RC - LEAD) + lax.broadcasted_iota(jnp.int32, (RC, 128), 0)
        den = jnp.ones((RC, 128), jnp.float32)
        for c in range(CLS_LOC):
            here = (place >= c * ROTS) & (place < (c + 1) * ROTS)
            den = jnp.where(here, jnp.broadcast_to(mass[:, c:c + 1], (RC, 128)), den)
        g_ref[ch, y, z] = (num / den).astype(jnp.bfloat16)
        for k in (4, 3, 5, 2, 6, 1, 7):
            zg[ch, k] = send(g_ref.at[ch, y, z], g_ref.at[ch, y, z],
                             zsend.at[ch, 6 + k], zrecv.at[ch, 6 + k], zdev[k])

    def share(ch):
        for k in range(1, 8):
            zg[ch, k].wait_recv()
        m7[ch] = send(g_ref.at[ch, y], g_ref.at[ch, y], ysend.at[ch, 6], yrecv.at[ch, 6], up)
        m8[ch] = send(g_ref.at[ch, y], g_ref.at[ch, y], ysend.at[ch, 7], yrecv.at[ch, 7], down)

    def pass_on(ch):
        m7[ch].wait_recv()
        m9[ch] = send(g_ref.at[ch, ym, A], g_ref.at[ch, ym, A], ysend.at[ch, 8], yrecv.at[ch, 8], up)
        m8[ch].wait_recv()
        m10[ch] = send(g_ref.at[ch, yp, B], g_ref.at[ch, yp, B], ysend.at[ch, 9], yrecv.at[ch, 9], down)

    far(0)
    near(0)
    for step in range(NCH + 4):
        if step + 1 < NCH:
            far(step + 1)
        for lag, stage in enumerate((relay, column, finish, share, pass_on)):
            if stage is column and step + 1 < NCH:
                near(step + 1)
            if 0 <= step - lag < NCH:
                stage(step - lag)
    for ch in range(NCH):
        m9[ch].wait_recv()
        m10[ch].wait_recv()
    for group in (m1, m2, m3, m4, m5, m6, zm, zg, m7, m8, m9, m10):
        for copy in group.values():
            copy.wait_send()


def reduce_average(payload):
    half = pltpu.VMEM((NCH, 4, RC, 128), jnp.bfloat16)
    return pl.pallas_call(
        reduce_kernel,
        out_shape=jax.ShapeDtypeStruct((NCH, 4, 8, RC, 128), jnp.bfloat16),
        in_specs=[pl.BlockSpec(memory_space=pltpu.VMEM)],
        out_specs=pl.BlockSpec(memory_space=pltpu.VMEM),
        scratch_shapes=[half] * 8 + [
            pltpu.VMEM((NCH, 8, RC, 128), jnp.bfloat16),
            pltpu.VMEM((NCH, 7, RC, 128), jnp.bfloat16),
            pltpu.SemaphoreType.DMA((NCH, 10)),
            pltpu.SemaphoreType.DMA((NCH, 10)),
            pltpu.SemaphoreType.DMA((NCH, 14)),
            pltpu.SemaphoreType.DMA((NCH, 14)),
        ],
        compiler_params=pltpu.CompilerParams(collective_id=5, has_side_effects=True, vmem_limit_bytes=40 << 20),
        name="reduce_average",
    )(payload)


def unpack_average(gathered):
    rows = gathered.transpose(1, 0, 3, 2, 4).reshape(4, NCH * RC, 8, 128)[:, LEAD:]
    return rows.reshape(CLS_LOC, 36864)


def in_hbm(*arrays):
    return [pltpu.with_memory_space_constraint(array, pltpu.HBM) for array in arrays]


def shards(particles, references, candidates, offsets):
    unit = jnp.asarray(unit_tables())
    images, cands, priors, refs, powers = gather_particles(
        particles.reshape(PART, 288, 128), *in_hbm(candidates, offsets.T, references), unit)
    scores, moved, stats, table = score_slots(cands, priors, powers, images, refs)
    payload = sum_slots(table, normalise(stats), scores, moved)
    return unpack_average(reduce_average(payload))


def solution(mesh):
    in_specs = (
        P(("cls", "dom"), None),
        P("cls", None),
        P(("cls", "dom"), None),
        P(("cls", "dom"), None),
    )
    return jax.shard_map(shards, mesh=mesh, in_specs=in_specs, out_specs=P("cls", None), check_vma=False)
```

```python
import math
import numpy as np
import jax, jax.numpy as jnp
from jax import lax
from jax.experimental import pallas as pl
from jax.experimental.pallas import tpu as pltpu
from jax.sharding import PartitionSpec as P

MESH = pl.DeviceIdType.MESH
CYCLES, ANGLES, ROTS, SHIFTS, BOX = 128, 144, 36, 5, 256
CLS_LOC, NCH, RC, LEAD, DROWS = 25, 5, 48, 15, 225
GROUPS, SLOTS, PART = 8, 16, 4
NEGATIVE = -1e30
WIDTH, LHS_ROWS, ACC_ROWS = 1024, 48, 40


def unit_tables():
    angle = 2.0 * math.pi * np.arange(ANGLES) / ANGLES
    radius = np.arange(1, CYCLES + 1)
    out = np.zeros((2, 2, 4, ACC_ROWS, CYCLES), np.float64)
    for axis, along in enumerate((np.cos(angle), np.sin(angle))):
        phase = (2.0 * math.pi / BOX) * along[:, None] * radius
        for part, value in enumerate((np.cos(phase), np.sin(phase))):
            out[axis, part, :, :ROTS] = value.reshape(ROTS, 4, CYCLES).transpose(1, 0, 2)
    return out.astype(np.float32)


def gather_kernel(p_ref, cand_ref, offs_ref, refs_ref, unit_ref, out_ref, cout_ref, oout_ref, rows_ref, powers, flat, unit, tall, lsem, ssem, rsem):
    me = lax.axis_index("cls")
    core = me % 2
    right, left, across = (me + 2) % GROUPS, (me + 6) % GROUPS, (me + 4) % GROUPS
    pair = me + 1 - 2 * core
    shift = pair - me
    barrier = pltpu.get_barrier_semaphore()
    for k in range(1, GROUPS):
        pl.semaphore_signal(barrier, inc=1, device_id={"cls": (me + k) % GROUPS}, device_id_type=MESH)
    pl.semaphore_wait(barrier, GROUPS - 1)
    h0, h1 = pl.ds(0, 2), pl.ds(2, 2)
    sends = []

    def send(src, dst, i, target):
        copy = pltpu.make_async_remote_copy(src_ref=src, dst_ref=dst, send_sem=ssem.at[i], recv_sem=rsem.at[i],
                                            device_id={"cls": target}, device_id_type=MESH)
        copy.start()
        sends.append(copy)
        return copy

    metas = [send(cand_ref, cout_ref.at[me], 12 + k, (me + k) % GROUPS) for k in range(1, GROUPS)]
    metas += [send(offs_ref, oout_ref.at[me], 19 + k, (me + k) % GROUPS) for k in range(1, GROUPS)]
    r0 = send(p_ref.at[h0], out_ref.at[me, h0], 0, right)
    l1 = send(p_ref.at[h1], out_ref.at[me, h1], 1, left)
    r1 = send(p_ref.at[h1], out_ref.at[me, h1], 2, right)
    l0 = send(p_ref.at[h0], out_ref.at[me, h0], 3, left)
    own = send(p_ref, out_ref.at[me], 4, pair)
    locals_ = [pltpu.make_async_copy(p_ref, out_ref.at[me], lsem.at[0]),
               pltpu.make_async_copy(cand_ref, cout_ref.at[me], lsem.at[1]),
               pltpu.make_async_copy(offs_ref, oout_ref.at[me], lsem.at[2])]
    fetch = pltpu.make_async_copy(refs_ref, flat, lsem.at[3])
    fetch.start()
    fetch_unit = pltpu.make_async_copy(unit_ref, unit, lsem.at[4])
    fetch_unit.start()
    for copy in locals_:
        copy.start()

    def clear(c, carry):
        for g in range(8):
            tall[g, pl.ds(pl.multiple_of(c * LHS_ROWS + 32, 16), 16), :] = jnp.zeros((16, 128), jnp.float32)
        return carry

    def spread(l, carry):
        value = flat[:, pl.ds(pl.multiple_of(l * WIDTH, WIDTH), WIDTH)].astype(jnp.float32)
        for g in range(8):
            tall[g, pl.ds(ROTS - 1 - l, CLS_LOC, stride=LHS_ROWS), :] = value[:, 128 * g:128 * g + 128]
        return carry

    def pack(c, carry):
        rows = pl.ds(pl.multiple_of(c * LHS_ROWS, LHS_ROWS), LHS_ROWS)
        for g in range(8):
            rows_ref[c, :, 128 * g:128 * g + 128] = tall[g, rows, :].astype(jnp.bfloat16)
        return carry

    lax.fori_loop(0, CLS_LOC, clear, 0)
    fetch.wait()
    lax.fori_loop(0, ROTS, spread, 0)
    r0.wait_recv()
    fr = send(out_ref.at[left, h0], out_ref.at[left, h0], 5, right)
    s0 = send(out_ref.at[left, h0], out_ref.at[left, h0], 7, pair)
    l1.wait_recv()
    fl = send(out_ref.at[right, h1], out_ref.at[right, h1], 6, left)
    s1 = send(out_ref.at[right, h1], out_ref.at[right, h1], 8, pair)
    lax.fori_loop(0, CLS_LOC, pack, 0)
    fetch_unit.wait()
    for axis in range(2):
        powers[axis, 0, 0] = jnp.ones((4, ACC_ROWS, 128), jnp.float32)
        powers[axis, 0, 1] = jnp.zeros((4, ACC_ROWS, 128), jnp.float32)
        powers[axis, 1] = unit[axis]
        for t in range(2, 8):
            pc, ps = powers[axis, t - 1, 0], powers[axis, t - 1, 1]
            qc, qs = unit[axis, 0], unit[axis, 1]
            powers[axis, t, 0] = pc * qc - ps * qs
            powers[axis, t, 1] = ps * qc + pc * qs
    r1.wait_recv()
    s2 = send(out_ref.at[left, h1], out_ref.at[left, h1], 9, pair)
    l0.wait_recv()
    s3 = send(out_ref.at[right, h0], out_ref.at[right, h0], 10, pair)
    fr.wait_recv()
    s4 = send(out_ref.at[across, h0], out_ref.at[across, h0], 11, pair)
    fl.wait_recv()
    s5 = send(out_ref.at[across, h1], out_ref.at[across, h1], 12, pair)
    for copy in [own, s0, s1, s2, s3, s4, s5] + metas:
        copy.wait_recv()
    for copy in locals_:
        copy.wait()
    for copy in sends:
        copy.wait_send()


def gather_particles(images, candidates, offsets, refs, unit):
    vmem = pl.BlockSpec(memory_space=pltpu.VMEM)
    return pl.pallas_call(
        gather_kernel,
        out_shape=(jax.ShapeDtypeStruct((GROUPS, PART, 288, 128), jnp.bfloat16),
                   jax.ShapeDtypeStruct((GROUPS, PART, 8), jnp.int32),
                   jax.ShapeDtypeStruct((GROUPS, 2, PART), jnp.int32),
                   jax.ShapeDtypeStruct((CLS_LOC, LHS_ROWS, WIDTH), jnp.bfloat16),
                   jax.ShapeDtypeStruct((2, 8, 2, 4, ACC_ROWS, 128), jnp.float32)),
        in_specs=[vmem] + [pl.BlockSpec(memory_space=pltpu.HBM)] * 4,
        out_specs=(vmem,) * 5,
        scratch_shapes=[pltpu.VMEM((CLS_LOC, ROTS * WIDTH), jnp.bfloat16),
                        pltpu.VMEM((2, 2, 4, ACC_ROWS, 128), jnp.float32), pltpu.VMEM((8, CLS_LOC * LHS_ROWS, 128), jnp.float32), pltpu.SemaphoreType.DMA((5,)),
                        pltpu.SemaphoreType.DMA((27,)), pltpu.SemaphoreType.DMA((27,))],
        compiler_params=pltpu.CompilerParams(collective_id=1, has_side_effects=True, vmem_limit_bytes=24 << 20),
        name="gather_particles",
    )(images, candidates, offsets, refs, unit)


def group_turn(lane):
    return lane - jnp.where(lane >= 80, 80, jnp.where(lane >= 40, 40, 0))


def lane_places(rows):
    row = lax.broadcasted_iota(jnp.int32, (rows, 128), 0)
    lane = lax.broadcasted_iota(jnp.int32, (rows, 128), 1)
    return row, lane, group_turn(lane)


def score_kernel(cands, priors, powers, images, refs, scores, moved, stats, table, wide):
    owner = lax.axis_index("cls")
    base = jnp.int32(0)
    for pid in range(GROUPS * PART):
        spot = base
        for t in range(8):
            c = cands[pid // PART, pid % PART, t] - owner * CLS_LOC
            table[spot] = c
            spot = spot + jnp.where(c.astype(jnp.uint32) < CLS_LOC, 1, 0)
        table[base + 6] = pid
        base = base + jnp.where(spot > base, 8, 0)
    place = base // 8
    table[SLOTS * 8 + 7] = place
    wide[288:320, :] = jnp.zeros((32, 128), jnp.float32)
    first = lax.broadcasted_iota(jnp.int32, (8, 128), 0) == 0
    stats[...] = jnp.where(first, NEGATIVE, 0.0)

    def one_slot(slot, carry):
        pid = table[slot * 8 + 6]
        v, i = pid // PART, pid % PART
        tx, ty = priors[v, 0, i], priors[v, 1, i]
        ax, ay = jnp.abs(tx), jnp.abs(ty)
        gx = jnp.where(tx < 0, -1.0, 1.0).astype(jnp.float32)
        gy = jnp.where(ty < 0, -1.0, 1.0).astype(jnp.float32)
        wide[0:288, :] = images[v, i].astype(jnp.float32)
        gap8, gap48 = jnp.zeros((8, 128), jnp.float32), jnp.zeros((48, 128), jnp.float32)
        for a in range(4):
            re = wide[pl.ds(2 * a, ACC_ROWS, stride=8), :]
            im = wide[pl.ds(2 * a + 1, ACC_ROWS, stride=8), :]
            cx, sx = powers[0, ax, 0, a], powers[0, ax, 1, a] * gx
            cy, sy = powers[1, ay, 0, a], powers[1, ay, 1, a] * gy
            bc, bs = cx * cy - sx * sy, sx * cy + cx * sy
            zr, zi = re * bc + im * bs, im * bc - re * bs
            real, imag = [zr], [zi]
            for axis in range(2):
                uc, us = powers[axis, 1, 0, a], powers[axis, 1, 1, a]
                rc, rs, ic, js = zr * uc, zr * us, zi * uc, zi * us
                real += [rc + js, rc - js]
                imag += [ic - rs, ic + rs]
            for m, part in enumerate((real, imag)):
                lanes = pl.ds(256 * a + 128 * m, 128)
                moved[slot, 0:128, lanes] = jnp.concatenate(part[0:3] + [gap8], axis=0).astype(jnp.bfloat16)
                moved[slot, 128:256, lanes] = jnp.concatenate(part[3:5] + [gap48], axis=0).astype(jnp.bfloat16)
        lhs = jnp.concatenate([refs[table[slot * 8 + k]] for k in range(4)], axis=0)
        pairs = lax.dot_general(lhs, moved[slot], (((1,), (1,)), ((), ())), preferred_element_type=jnp.float32)
        row = lax.broadcasted_iota(jnp.int32, (ACC_ROWS, 128), 0)
        lane = lax.broadcasted_iota(jnp.int32, (ACC_ROWS, 128), 1)
        turn = group_turn(jnp.where(lane >= ROTS - 1, lane - (ROTS - 1), lane + 128 - (ROTS - 1)))
        turn2 = group_turn(jnp.where(lane == 127, 0, lane + 1))
        back = (ROTS - 1) - row
        direct = (turn + back < ROTS) & (back >= 0)
        wrapped = (turn2 < ROTS) & (turn2 + back >= ROTS)
        _, lane1, turn1 = lane_places(8)
        lines = []
        for half in range(2):
            rows = []
            for k in range(4):
                block = pairs[LHS_ROWS * k:LHS_ROWS * k + ACC_ROWS, 128 * half:128 * half + 128]
                skew = pltpu.roll(block, 0, 1, stride=1, stride_axis=0)
                near = jnp.sum(jnp.where(direct, skew, 0.0), axis=0, keepdims=True)
                far = jnp.sum(jnp.where(wrapped, skew, 0.0), axis=0, keepdims=True)
                rows.append((near, far))
            near = jnp.concatenate([r[0] for r in rows] + [jnp.zeros((4, 128), jnp.float32)], axis=0)
            far = jnp.concatenate([r[1] for r in rows] + [jnp.zeros((4, 128), jnp.float32)], axis=0)
            whole = 2.0 * (pltpu.roll(near, 128 - (ROTS - 1), 1) + pltpu.roll(far, 1, 1))
            row8 = lax.broadcasted_iota(jnp.int32, (8, 128), 0)
            good = (turn1 < ROTS) & (lane1 < (120 if half == 0 else 80)) & (row8 < 4)
            line = jnp.where(good, whole, NEGATIVE)
            scores[slot, :, 128 * half:128 * half + 128] = line
            lines.append(line)
        best = jnp.max(jnp.max(jnp.maximum(lines[0], lines[1]), axis=1, keepdims=True), axis=0, keepdims=True)
        power = jnp.exp(lines[0] - best) + jnp.exp(lines[1] - best)
        mass = jnp.sum(jnp.sum(power, axis=1, keepdims=True), axis=0, keepdims=True)
        here = lax.broadcasted_iota(jnp.int32, (1, 128), 1) == pid
        stats[0:1, :] = jnp.where(here, best, stats[0:1, :])
        stats[1:2, :] = jnp.where(here, mass, stats[1:2, :])
        return carry

    lax.fori_loop(0, place, one_slot, 0)


def score_slots(cands, priors, powers, images, refs):
    vmem, smem = pl.BlockSpec(memory_space=pltpu.VMEM), pl.BlockSpec(memory_space=pltpu.SMEM)
    return pl.pallas_call(
        score_kernel,
        out_shape=(jax.ShapeDtypeStruct((SLOTS, 8, 256), jnp.float32),
                   jax.ShapeDtypeStruct((SLOTS, 256, WIDTH), jnp.bfloat16),
                   jax.ShapeDtypeStruct((8, 128), jnp.float32),
                   jax.ShapeDtypeStruct(((SLOTS + 1) * 8,), jnp.int32)),
        in_specs=[smem, smem, vmem, vmem, vmem],
        out_specs=(vmem, vmem, vmem, smem),
        scratch_shapes=[pltpu.VMEM((320, 128), jnp.float32)],
        compiler_params=pltpu.CompilerParams(vmem_limit_bytes=32 << 20),
        name="score_slots",
    )(cands, priors, powers, images, refs)


def norm_kernel(stats, total, boxes, ssem, rsem):
    me = lax.axis_index("cls")
    barrier = pltpu.get_barrier_semaphore()
    for k in range(1, GROUPS):
        pl.semaphore_signal(barrier, inc=1, device_id={"cls": (me + k) % GROUPS}, device_id_type=MESH)
    pl.semaphore_wait(barrier, GROUPS - 1)
    copies = []
    for k in range(1, GROUPS):
        copy = pltpu.make_async_remote_copy(src_ref=stats, dst_ref=boxes.at[k - 1], send_sem=ssem.at[k - 1],
                                            recv_sem=rsem.at[k - 1], device_id={"cls": (me + k) % GROUPS},
                                            device_id_type=MESH)
        copy.start()
        copies.append(copy)
    for copy in copies:
        copy.wait_recv()
    best = stats[0:1, :]
    for k in range(GROUPS - 1):
        best = jnp.maximum(best, boxes[k, 0:1, :])
    whole = stats[1:2, :] * jnp.exp(stats[0:1, :] - best)
    for k in range(GROUPS - 1):
        whole = whole + boxes[k, 1:2, :] * jnp.exp(boxes[k, 0:1, :] - best)
    total[...] = jnp.concatenate([best, whole, jnp.zeros((6, 128), jnp.float32)], axis=0)
    for copy in copies:
        copy.wait_send()


def normalise(stats):
    vmem = pl.BlockSpec(memory_space=pltpu.VMEM)
    return pl.pallas_call(
        norm_kernel,
        out_shape=jax.ShapeDtypeStruct((8, 128), jnp.float32),
        in_specs=[vmem],
        out_specs=vmem,
        scratch_shapes=[pltpu.VMEM((GROUPS - 1, 8, 128), jnp.float32),
                        pltpu.SemaphoreType.DMA((7,)), pltpu.SemaphoreType.DMA((7,))],
        compiler_params=pltpu.CompilerParams(collective_id=2, has_side_effects=True, vmem_limit_bytes=4 << 20),
        name="normalise",
    )(stats)


def sum_kernel(table, total, scores, moved, out, acc, comp, masses, spread):
    filled = table[SLOTS * 8 + 7]
    acc[...] = jnp.zeros(acc.shape, jnp.float32)
    masses[...] = jnp.zeros(masses.shape, jnp.float32)

    def prepare(slot, count):
        pid = table[slot * 8 + 6]
        place = lax.broadcasted_iota(jnp.int32, (1, 128), 1) == pid
        best = jnp.sum(jnp.where(place, total[0:1, :], 0.0), axis=1, keepdims=True)
        whole = jnp.sum(jnp.where(place, total[1:2, :], 0.0), axis=1, keepdims=True)
        row, _, turn = lane_places(ACC_ROWS)
        later = turn >= row
        halves = []
        mass = jnp.zeros((8, 1), jnp.float32)
        for half in range(2):
            weight = jnp.exp(scores[slot, :, 128 * half:128 * half + 128] - best) / whole
            weight = weight.astype(jnp.bfloat16).astype(jnp.float32)
            mass = mass + jnp.sum(weight, axis=1, keepdims=True)
            back = pltpu.roll(weight, 92, 1)
            rows = []
            for k in range(4):
                one = jnp.broadcast_to(weight[k:k + 1, :], (ACC_ROWS, 128))
                two = jnp.broadcast_to(back[k:k + 1, :], (ACC_ROWS, 128))
                rows.append(jnp.where(later, pltpu.roll(one, 0, 1, stride=1, stride_axis=0),
                                      pltpu.roll(two, 0, 1, stride=1, stride_axis=0)))
            halves.append(jnp.concatenate(rows, axis=0))
        spread[slot % 2] = jnp.concatenate(halves, axis=1).astype(jnp.bfloat16)
        for k in range(4):
            c = table[slot * 8 + k]
            masses[pl.ds(c, 1), :] = masses[pl.ds(c, 1), :] + count * jnp.broadcast_to(mass[k:k + 1, :], (1, 128))

    def one_slot(slot, carry):
        contrib = jnp.dot(spread[slot % 2], moved[slot], preferred_element_type=jnp.float32)
        prepare(jnp.minimum(slot + 1, filled - 1), jnp.where(slot + 1 < filled, 1.0, 0.0))
        for k in range(4):
            c = table[slot * 8 + k]
            acc[c] = acc[c] + contrib[ACC_ROWS * k:ACC_ROWS * (k + 1)]
        return carry

    @pl.when(filled > 0)
    def _():
        prepare(0, 1.0)
        lax.fori_loop(0, filled, one_slot, 0)

    row = lax.broadcasted_iota(jnp.int32, (32, 128), 0)
    lane = lax.broadcasted_iota(jnp.int32, (32, 128), 1)
    line = jnp.sum(jnp.where(row == lane, masses[...], 0.0), axis=0, keepdims=True)
    high = line.astype(jnp.bfloat16).astype(jnp.float32)
    lead = jnp.concatenate([high, line - high, jnp.zeros((14, 128), jnp.float32)], axis=0)
    for y in range(4):
        comp[y * 240:y * 240 + 16, :] = jnp.concatenate([lead] * 8, axis=1)
    for c in range(CLS_LOC):
        start = c * ROTS
        while start < (c + 1) * ROTS:
            y = start // DROWS
            stop = min((c + 1) * ROTS, (y + 1) * DROWS)
            to = y * 240 + LEAD + start - y * DROWS
            comp[to:to + stop - start, :] = acc[c, start - c * ROTS:stop - c * ROTS, :]
            start = stop
    for ch in range(NCH):
        for y in range(4):
            for z in range(8):
                out[ch, y, z] = comp[y * 240 + ch * RC:y * 240 + (ch + 1) * RC,
                                     128 * z:128 * z + 128].astype(jnp.bfloat16)


def sum_slots(table, total, scores, moved):
    vmem, smem = pl.BlockSpec(memory_space=pltpu.VMEM), pl.BlockSpec(memory_space=pltpu.SMEM)
    return pl.pallas_call(
        sum_kernel,
        out_shape=jax.ShapeDtypeStruct((NCH, 4, 8, RC, 128), jnp.bfloat16),
        in_specs=[smem, vmem, vmem, vmem],
        out_specs=vmem,
        scratch_shapes=[pltpu.VMEM((CLS_LOC, ACC_ROWS, WIDTH), jnp.float32),
                        pltpu.VMEM((960, WIDTH), jnp.float32),
                        pltpu.VMEM((32, 128), jnp.float32),
                        pltpu.VMEM((2, 4 * ACC_ROWS, 256), jnp.bfloat16)],
        compiler_params=pltpu.CompilerParams(vmem_limit_bytes=32 << 20),
        name="sum_slots",
    )(table, total, scores, moved)


def reduce_kernel(p_ref, g_ref, x1, x2, d3, d4, e5, e6, c1, c2, s_buf, z_buf, ysend, yrecv, zsend, zrecv):
    dom = lax.axis_index("dom")
    y = dom % 4
    z = dom // 4
    yp, ym, yo = (y + 1) % 4, (y + 3) % 4, (y + 2) % 4
    up, down = {"dom": z * 4 + yp}, {"dom": z * 4 + ym}
    zdev = [{"dom": ((z + k) % 8) * 4 + y} for k in range(8)]
    barrier = pltpu.get_barrier_semaphore()
    for target in [up, down] + zdev[1:]:
        pl.semaphore_signal(barrier, inc=1, device_id=target, device_id_type=MESH)
    pl.semaphore_wait(barrier, 9)
    A, B = pl.ds(0, 4), pl.ds(4, 4)

    def send(src, dst, ssem, rsem, target):
        copy = pltpu.make_async_remote_copy(src_ref=src, dst_ref=dst, send_sem=ssem, recv_sem=rsem,
                                            device_id=target, device_id_type=MESH)
        copy.start()
        return copy

    m1, m2, m3, m4, m5, m6 = {}, {}, {}, {}, {}, {}
    zm, zg, m7, m8, m9, m10 = {}, {}, {}, {}, {}, {}
    masses = []

    def far(ch):
        m1[ch] = send(p_ref.at[ch, yo, A], x1.at[ch], ysend.at[ch, 0], yrecv.at[ch, 0], up)
        m2[ch] = send(p_ref.at[ch, yo, B], x2.at[ch], ysend.at[ch, 1], yrecv.at[ch, 1], down)

    def near(ch):
        m3[ch] = send(p_ref.at[ch, yp, B], d3.at[ch], ysend.at[ch, 2], yrecv.at[ch, 2], up)
        m4[ch] = send(p_ref.at[ch, ym, A], d4.at[ch], ysend.at[ch, 3], yrecv.at[ch, 3], down)

    def relay(ch):
        m1[ch].wait_recv()
        c1[ch] = (x1[ch].astype(jnp.float32) + p_ref[ch, yp, A].astype(jnp.float32)).astype(jnp.bfloat16)
        m5[ch] = send(c1.at[ch], e5.at[ch], ysend.at[ch, 4], yrecv.at[ch, 4], up)
        m2[ch].wait_recv()
        c2[ch] = (x2[ch].astype(jnp.float32) + p_ref[ch, ym, B].astype(jnp.float32)).astype(jnp.bfloat16)
        m6[ch] = send(c2.at[ch], e6.at[ch], ysend.at[ch, 5], yrecv.at[ch, 5], down)

    def column(ch):
        m4[ch].wait_recv()
        m5[ch].wait_recv()
        s_buf[ch, A] = (p_ref[ch, y, A].astype(jnp.float32) + e5[ch].astype(jnp.float32)
                        + d4[ch].astype(jnp.float32)).astype(jnp.bfloat16)
        m3[ch].wait_recv()
        m6[ch].wait_recv()
        s_buf[ch, B] = (p_ref[ch, y, B].astype(jnp.float32) + e6[ch].astype(jnp.float32)
                        + d3[ch].astype(jnp.float32)).astype(jnp.bfloat16)
        for k in (4, 3, 5, 2, 6, 1, 7):
            zm[ch, k] = send(s_buf.at[ch, (z + k) % 8], z_buf.at[ch, k - 1],
                             zsend.at[ch, k - 1], zrecv.at[ch, k - 1], zdev[k])

    def finish(ch):
        num = s_buf[ch, z].astype(jnp.float32)
        for k in range(1, 8):
            zm[ch, k].wait_recv()
            num = num + z_buf[ch, k - 1].astype(jnp.float32)
        if ch == 0:
            masses.append(num[0:1, :] + num[1:2, :] + 1.0)
        mass = masses[0]
        place = DROWS * y + (ch * RC - LEAD) + lax.broadcasted_iota(jnp.int32, (RC, 128), 0)
        den = jnp.ones((RC, 128), jnp.float32)
        for c in range(CLS_LOC):
            here = (place >= c * ROTS) & (place < (c + 1) * ROTS)
            den = jnp.where(here, jnp.broadcast_to(mass[:, c:c + 1], (RC, 128)), den)
        g_ref[ch, y, z] = (num / den).astype(jnp.bfloat16)
        for k in (2, 6, 1, 7):
            hand(ch, k, z, k)

    def hand(ch, k, piece, to):
        zg[ch, k] = send(g_ref.at[ch, y, piece], g_ref.at[ch, y, piece],
                         zsend.at[ch, 6 + k], zrecv.at[ch, 6 + k], zdev[to])

    def forward(ch):
        below, above = (z + 6) % 8, (z + 2) % 8
        zg[ch, 2].wait_recv()
        if ch % 2 == 0:
            hand(ch, 4, below, 2)
        hand(ch, 3, below, 1)
        zg[ch, 6].wait_recv()
        if ch % 2 == 1:
            hand(ch, 4, above, 6)
        hand(ch, 5, above, 7)

    def share(ch):
        for k in (1, 7, 3, 4, 5):
            zg[ch, k].wait_recv()
        m7[ch] = send(g_ref.at[ch, y], g_ref.at[ch, y], ysend.at[ch, 6], yrecv.at[ch, 6], up)
        m8[ch] = send(g_ref.at[ch, y], g_ref.at[ch, y], ysend.at[ch, 7], yrecv.at[ch, 7], down)

    def pass_on(ch):
        m7[ch].wait_recv()
        m9[ch] = send(g_ref.at[ch, ym, A], g_ref.at[ch, ym, A], ysend.at[ch, 8], yrecv.at[ch, 8], up)
        m8[ch].wait_recv()
        m10[ch] = send(g_ref.at[ch, yp, B], g_ref.at[ch, yp, B], ysend.at[ch, 9], yrecv.at[ch, 9], down)

    far(0)
    near(0)
    for step in range(NCH + 5):
        if step + 1 < NCH:
            far(step + 1)
        for lag, stage in enumerate((relay, column, finish, forward, share, pass_on)):
            if stage is column and step + 1 < NCH:
                near(step + 1)
            if 0 <= step - lag < NCH:
                stage(step - lag)
    for ch in range(NCH):
        m9[ch].wait_recv()
        m10[ch].wait_recv()
    for group in (m1, m2, m3, m4, m5, m6, zm, zg, m7, m8, m9, m10):
        for copy in group.values():
            copy.wait_send()


def reduce_average(payload):
    half = pltpu.VMEM((NCH, 4, RC, 128), jnp.bfloat16)
    return pl.pallas_call(
        reduce_kernel,
        out_shape=jax.ShapeDtypeStruct((NCH, 4, 8, RC, 128), jnp.bfloat16),
        in_specs=[pl.BlockSpec(memory_space=pltpu.VMEM)],
        out_specs=pl.BlockSpec(memory_space=pltpu.VMEM),
        scratch_shapes=[half] * 8 + [
            pltpu.VMEM((NCH, 8, RC, 128), jnp.bfloat16),
            pltpu.VMEM((NCH, 7, RC, 128), jnp.bfloat16),
            pltpu.SemaphoreType.DMA((NCH, 10)),
            pltpu.SemaphoreType.DMA((NCH, 10)),
            pltpu.SemaphoreType.DMA((NCH, 14)),
            pltpu.SemaphoreType.DMA((NCH, 14)),
        ],
        compiler_params=pltpu.CompilerParams(collective_id=5, has_side_effects=True, vmem_limit_bytes=40 << 20),
        name="reduce_average",
    )(payload)


def unpack_average(gathered):
    rows = gathered.transpose(1, 0, 3, 2, 4).reshape(4, NCH * RC, 8, 128)[:, LEAD:]
    return rows.reshape(CLS_LOC, 36864)


def in_hbm(*arrays):
    return [pltpu.with_memory_space_constraint(array, pltpu.HBM) for array in arrays]


def shards(particles, references, candidates, offsets):
    unit = jnp.asarray(unit_tables())
    images, cands, priors, refs, powers = gather_particles(
        particles.reshape(PART, 288, 128), *in_hbm(candidates, offsets.T, references, unit))
    scores, moved, stats, table = score_slots(cands, priors, powers, images, refs)
    payload = sum_slots(table, normalise(stats), scores, moved)
    return unpack_average(reduce_average(payload))


def solution(mesh):
    in_specs = (
        P(("cls", "dom"), None),
        P("cls", None),
        P(("cls", "dom"), None),
        P(("cls", "dom"), None),
    )
    return jax.shard_map(shards, mesh=mesh, in_specs=in_specs, out_specs=P("cls", None), check_vma=False)
```
